512 devices in a mesh: plant: 8 (over z), feat: 8 (over x, core), samp: 8 (over y).
Axes of the slice: x: 4, y: 8, z: 8, core: 2. Of those that a mesh axis runs over, the one named last changes fastest.
Arguments:
- embeddings: bfloat16 [32768, 4096], P(('plant', 'samp'), 'feat'), may hold values from -6 to 6
- plant_ids: int32 [32768, 1], P(('plant', 'samp')), may hold values from 0 to 7; in each aligned block of 512 rows (0 to 511, 512 to 1023, ...) at most 128 rows name the same one
- labels: int32 [32768], P(('plant', 'samp')), may hold values from 0 to 1
- weights: float32 [8, 4096], P('plant', 'feat'), may hold values from -0.09375 to 0.09375
Outputs:
- newton_step: float32 [8, 4096], P('plant', ('feat', 'samp'))
- gradient: float32 [8, 4096], P('plant', ('feat', 'samp'))
The draws below stay inside these ranges and needn't reach their ends.
Inputs may be any that keep to these rules, and one draw needn't show every extreme that they name: `plant_ids`: in the 512 rows of one device no plant is named by more than 128 rows, a bound that some block reaches; every plant is named by some row.
All inputs are finite; a program needn't handle non-finite values.
Results may differ from the reference program's by a relative error of at most 0.0034.
Values may be sent and summed in bfloat16 or wider, within the bound.
No kernel may reach another device: no remote copies, remote signals or barrier semaphores. Data moves between devices by JAX's collectives and lax.ppermute only.
A program may use at most 64 MiB of HBM per device.

```python
import math
import jax
import jax.numpy as jnp
import numpy as np

D = 4096
ROWS_DEV = 512
ITERS = 2
PLANTS = 8
MOST = 128
NTOT = 32768


def with_ends(entries, stream_key, smallest, high):
    longest = entries.shape.index(max(entries.shape))
    spots = []
    for shift in (0, 1):
        where = [jax.random.randint(jax.random.fold_in(stream_key, axis), (), 0, length) for axis, length in enumerate(entries.shape)]
        where[longest] = (where[longest] + shift) % entries.shape[longest]
        spots.append(tuple(where))
    return entries.at[spots[0]].set(smallest).at[spots[1]].set(high)


def levels(own_key, extent, shards, low, top_value):
    factor_of = 1.0
    for axis_at, blocks in shards:
        steps = jax.random.uniform(jax.random.fold_in(jax.random.fold_in(own_key, 6), axis_at), (blocks,), jnp.float32, low / len(shards), top_value / len(shards))
        factor_of = factor_of * jnp.repeat(jnp.exp(steps), extent[axis_at] // blocks).reshape((-1,) + (1,) * (len(extent) - 1 - axis_at))
    return factor_of


def deal_out(own_key, own, number, rows, count, top, reach, slope):
    ranking = jax.random.permutation(own_key, count)
    crowded, ordinary = load_shares(count, rows * top, reach, slope, True), load_shares(count, rows * top, reach, slope, False)
    places = jnp.arange(count)

    def named(lengths, offset_by):
        used = int((lengths > 0).sum())
        fixed = max(1, used // 4)
        moved = fixed + (places - fixed + offset_by * (used - fixed)) % max(1, count - fixed)
        return jnp.zeros((count,), jnp.int32).at[ranking[jnp.where(places < fixed, places, moved)]].set(jnp.asarray(lengths, jnp.int32))

    lengths = jnp.where(number % 4 == 0, named(crowded, number // 4), named(ordinary, number - number // 4 - 1))
    mixed = jax.random.permutation(jax.random.fold_in(own, 3), count)
    source_of, sink = mixed[0:count // 2 * 2:2], mixed[1:count // 2 * 2:2]
    room = jnp.minimum(lengths[source_of] - 1, reach - lengths[sink]) // 2
    room = jnp.where((source_of == ranking[0]) | (sink == ranking[0]) | (lengths[sink] == 0), 0, jnp.maximum(room, 0))
    moved = jax.random.randint(jax.random.fold_in(own, 4), (count // 2,), 0, 1 << 20) % (room + 1)
    lengths = lengths.at[source_of].add(-moved).at[sink].add(moved)
    items = jnp.searchsorted(jnp.cumsum(lengths), jnp.arange(rows * top), side="right").astype(jnp.int32)
    listing = items.reshape(top, rows).T
    listing = listing[jax.random.permutation(jax.random.fold_in(own, 1), rows)]
    offset_by = jax.random.randint(jax.random.fold_in(own, 2), (rows, 1), 0, top)
    return jnp.take_along_axis(listing, (jnp.arange(top)[None, :] + offset_by) % top, axis=1)


def load_shares(count, total, limit, slope, full):
    weights = [(1 << 20) // math.isqrt(standing ** slope) + 1 for standing in range(1, count + 1)]
    largest = limit if full else min(limit, max(-(-total // count), total * weights[0] // sum(weights)))
    least = 1 if total - largest >= count - 1 else 0
    given, spare = [largest] + [least] * (count - 1), total - largest - least * (count - 1)
    while spare > 0:
        candidates = [i for i in range(1, count) if given[i] < largest] or [i for i in range(1, count) if given[i] < limit]
        mass, remaining = sum([weights[i] for i in candidates]), spare
        for i in candidates:
            extra = min(limit - given[i], max(1, remaining * weights[i] // mass), spare)
            given[i] = given[i] + extra
            spare = spare - extra
    return np.array(given)


def centred(stream_key, shape, spread, most, shards=(), held_as=jnp.bfloat16):
    drawn = jax.random.normal(stream_key, shape, jnp.float32) * spread
    if len(shards) > 0:
        drawn = levels(stream_key, shape, shards, -0.22, 0.18) * drawn
    return jnp.clip(drawn, min=-most, max=most).astype(held_as)


def setup_inputs(seed: int = 0) -> dict:
    seeds = jax.random.split(jax.random.key(seed), 5)
    embeddings = centred(seeds[0], (NTOT, D), 1.0, 6.0, ((0, 64), (1, 8)))
    plant_ids_keys = jax.random.split(jax.random.fold_in(seeds[1], 1), NTOT // ROWS_DEV)
    plant_ids_turns = jax.random.permutation(jax.random.fold_in(seeds[1], 3), NTOT // ROWS_DEV)
    plant_ids = jax.vmap(lambda own, number: deal_out(jax.random.fold_in(seeds[1], 2), own, number, ROWS_DEV, PLANTS, 1, MOST, 2))(plant_ids_keys, plant_ids_turns).reshape((NTOT, 1))
    labels = with_ends(jax.random.randint(seeds[2], (NTOT,), 0, 2), jax.random.fold_in(seeds[2], 1), 0, 1).astype(jnp.int32)
    weights = centred(seeds[3], (PLANTS, D), D ** -0.5, 0.09375, ((0, 8), (1, 8)), jnp.float32)
    return {"embeddings": embeddings, "plant_ids": plant_ids, "labels": labels, "weights": weights}


penalty = 0.1


def reference(embeddings, plant_ids, labels, weights):
    plant_col = plant_ids[:, 0]
    members = (plant_col[:, None] == jnp.arange(PLANTS, dtype=jnp.int32)[None, :]).astype(jnp.float32)
    counts = jnp.sum(members, axis=0)
    weights_bf = weights.astype(jnp.bfloat16)
    logits = jnp.sum(jnp.dot(embeddings, weights_bf.T, preferred_element_type=jnp.float32) * members, axis=1)
    prob_vals = jax.nn.sigmoid(logits)
    residual = prob_vals - labels.astype(jnp.float32)
    curvature = prob_vals * (1.0 - prob_vals)
    resid_rows = (members * residual[:, None]).astype(jnp.bfloat16)
    gradient = jnp.dot(resid_rows.T, embeddings, preferred_element_type=jnp.float32) / counts[:, None] + penalty * weights

    def hessian(direction):
        dir_bf = direction.astype(jnp.bfloat16)
        proj = jnp.sum(jnp.dot(embeddings, dir_bf.T, preferred_element_type=jnp.float32) * members, axis=1)
        weighted = (members * (curvature * proj)[:, None]).astype(jnp.bfloat16)
        return jnp.dot(weighted.T, embeddings, preferred_element_type=jnp.float32) / counts[:, None] + penalty * direction

    newton_step = jnp.zeros_like(gradient)
    resid_vec = -gradient
    direction = resid_vec
    sq_norm = jnp.sum(resid_vec * resid_vec, axis=1, keepdims=True)
    for iteration in range(ITERS):
        curv_image = hessian(direction)
        step_len = sq_norm / jnp.sum(direction * curv_image, axis=1, keepdims=True)
        newton_step = newton_step + step_len * direction
        if iteration + 1 < ITERS:
            resid_vec = resid_vec - step_len * curv_image
            sq_next = jnp.sum(resid_vec * resid_vec, axis=1, keepdims=True)
            direction = resid_vec + (sq_next / sq_norm) * direction
            sq_norm = sq_next
    return newton_step, gradient
```

```python
import functools

import jax
import jax.numpy as jnp
from jax import lax
from jax.experimental import pallas as pl
from jax.experimental.pallas import tpu as pltpu
from jax.sharding import PartitionSpec as P

penalty = 0.1
PEERS = 8
LANES = 128
f32 = jnp.float32
bf16 = jnp.bfloat16


def nt(a, b):
    return lax.dot_general(a, b, (((1,), (1,)), ((), ())), preferred_element_type=f32)


def nn(a, b):
    return lax.dot_general(a, b, (((1,), (0,)), ((), ())), preferred_element_type=f32)


def rep(row):
    return jnp.broadcast_to(row, (PEERS, row.shape[1]))


def lane0(ref, at):
    return jnp.sum(ref[:, at : at + LANES], axis=0, keepdims=True)[:, :1]


def call(kernel, *args, out):
    return pl.pallas_call(
        kernel,
        out_shape=out,
        in_specs=[pl.BlockSpec(memory_space=pltpu.VMEM)] * len(args),
        out_specs=jax.tree.map(lambda _: pl.BlockSpec(memory_space=pltpu.VMEM), out),
        name=kernel.func.__name__ if isinstance(kernel, functools.partial) else kernel.__name__,
    )(*args)


def shape(*dims, dtype=f32):
    return jax.ShapeDtypeStruct(dims, dtype)


def pack_rows(cap, ids_ref, lab_ref, emb_ref, out_ref):
    rows = emb_ref.shape[0]
    ids = ids_ref[...]
    heads = lax.broadcasted_iota(jnp.int32, (PEERS, rows), 0)
    members = heads == ids
    mem_f = members.astype(f32)
    earlier = lax.broadcasted_iota(jnp.int32, (rows, rows), 0) < lax.broadcasted_iota(
        jnp.int32, (rows, rows), 1
    )
    before = nn(mem_f.astype(bf16), earlier.astype(f32).astype(bf16))
    rank = jnp.sum(before * mem_f, axis=0, keepdims=True).astype(jnp.int32)
    at_rank = lax.broadcasted_iota(jnp.int32, (cap, rows), 0) == rank
    tags = (lab_ref[...] + 1).astype(f32)
    tag_slots = nt((mem_f * tags).astype(bf16), at_rank.astype(f32).astype(bf16))
    emb = emb_ref[...]
    for p in range(PEERS):
        pick = (at_rank & (ids == p)).astype(f32).astype(bf16)
        out_ref[p, :cap, :] = nn(pick, emb).astype(bf16)
        out_ref[p, cap:, :cap] = jnp.broadcast_to(tag_slots[p : p + 1], (PEERS, cap)).astype(bf16)
        out_ref[p, cap:, cap:] = jnp.zeros((PEERS, rows - cap), bf16)


def take_rows(cap, got_ref, w_ref, rows_ref, tags_ref, out_ref):
    for p in range(PEERS):
        rows_ref[p * cap : (p + 1) * cap, :] = got_ref[p, :cap, :]
        tags_ref[:, p * cap : (p + 1) * cap] = got_ref[p, cap:, :cap].astype(f32)
    out_ref[...] = nt(rep(w_ref[...]).astype(bf16), rows_ref[...])


def to_residual(got_ref, tags_ref, rows_ref, curv_ref, out_ref):
    width = rows_ref.shape[1]
    logits = jnp.sum(got_ref[...], axis=0, keepdims=True)
    tags = tags_ref[0:1, :]
    valid = tags > 0.0
    prob = jax.nn.sigmoid(logits)
    residual = jnp.where(valid, prob - jnp.maximum(tags - 1.0, 0.0), 0.0)
    curv_ref[...] = rep(jnp.where(valid, prob * (1.0 - prob), 0.0))
    out_ref[:, :width] = nn(rep(residual).astype(bf16), rows_ref[...])
    count = jnp.sum(valid.astype(f32), axis=1, keepdims=True)
    out_ref[:, width:] = jnp.broadcast_to(count, (PEERS, LANES))


def to_direction(got_ref, w_ref, rows_ref, grad_ref, count_ref, out_ref):
    width, slots = rows_ref.shape[1], rows_ref.shape[0]
    count = lane0(got_ref, width)
    grad = jnp.sum(got_ref[:, :width], axis=0, keepdims=True) / count + penalty * w_ref[...]
    grad_ref[...] = grad
    count_ref[...] = jnp.broadcast_to(count, (1, LANES))
    out_ref[:, :slots] = nt(rep(-grad).astype(bf16), rows_ref[...])
    out_ref[:, slots:] = jnp.broadcast_to(
        jnp.sum(grad * grad, axis=1, keepdims=True), (PEERS, LANES)
    )


def to_image(got_ref, curv_ref, rows_ref, proj_ref, out_ref):
    width, slots = rows_ref.shape[1], rows_ref.shape[0]
    total = jnp.sum(got_ref[...], axis=0, keepdims=True)
    proj_ref[...] = total
    proj = total[:, :slots]
    weighted = (curv_ref[0:1, :] * proj).astype(bf16)
    out_ref[:, :width] = nn(rep(weighted.astype(f32)).astype(bf16), rows_ref[...])
    bent = jnp.sum(weighted.astype(f32) * proj, axis=1, keepdims=True)
    out_ref[:, width:] = jnp.broadcast_to(bent, (PEERS, LANES))


def to_second(got_ref, proj_ref, grad_ref, count_ref, rows_ref, keep_ref, out_ref):
    width, slots = rows_ref.shape[1], rows_ref.shape[0]
    count = count_ref[:, :1]
    sq_norm = proj_ref[:, slots : slots + 1]
    direction = -grad_ref[...]
    image = jnp.sum(got_ref[:, :width], axis=0, keepdims=True) / count + penalty * direction
    step = sq_norm / (lane0(got_ref, width) / count + penalty * sq_norm)
    resid = direction - step * image
    keep_ref[:, :width] = resid
    keep_ref[:, width:] = jnp.broadcast_to(step, (1, LANES))
    out_ref[:, :slots] = nt(rep(resid).astype(bf16), rows_ref[...])
    out_ref[:, slots : slots + LANES] = jnp.broadcast_to(
        jnp.sum(resid * resid, axis=1, keepdims=True), (PEERS, LANES)
    )
    out_ref[:, slots + LANES :] = jnp.broadcast_to(
        jnp.sum(resid * direction, axis=1, keepdims=True), (PEERS, LANES)
    )


def to_bend(got_ref, proj_ref, curv_ref, keep_ref, out_ref):
    slots = curv_ref.shape[1]
    total = jnp.sum(got_ref[...], axis=0, keepdims=True)
    sq_norm = proj_ref[:, slots : slots + 1]
    sq_next = total[:, slots : slots + 1]
    cross = total[:, slots + LANES : slots + LANES + 1]
    beta = sq_next / sq_norm
    proj = total[:, :slots] + beta * proj_ref[:, :slots]
    weighted = (curv_ref[0:1, :] * proj).astype(bf16).astype(f32)
    out_ref[...] = jnp.broadcast_to(
        jnp.sum(weighted * proj, axis=1, keepdims=True), (PEERS, LANES)
    )
    dir_sq = sq_next + 2.0 * beta * cross + beta * beta * sq_norm
    keep_ref[0:1, :] = jnp.broadcast_to(beta, (1, LANES))
    keep_ref[1:2, :] = jnp.broadcast_to(sq_next, (1, LANES))
    keep_ref[2:3, :] = jnp.broadcast_to(dir_sq, (1, LANES))
    keep_ref[3:, :] = jnp.zeros((PEERS - 3, LANES), f32)


def to_step(got_ref, count_ref, keep_ref, first_ref, grad_ref, resid_ref, out_ref):
    beta, sq_next, dir_sq = keep_ref[0:1, :1], keep_ref[1:2, :1], keep_ref[2:3, :1]
    step = sq_next / (lane0(got_ref, 0) / count_ref[:, :1] + penalty * dir_sq)
    direction = -grad_ref[...]
    out_ref[...] = first_ref[:, :1] * direction + step * (resid_ref[...] + beta * direction)


def exchange(values, axis):
    return lax.all_to_all(values, axis, split_axis=0, concat_axis=0, tiled=True)


def shards(embeddings, plant_ids, labels, weights):
    rows_here, width = embeddings.shape
    samps = lax.axis_size("samp")
    share = width // samps
    cap = 2 * rows_here // PEERS
    slots = PEERS * cap
    at = lax.axis_index("samp") * share

    sent = call(
        functools.partial(pack_rows, cap),
        plant_ids.reshape(1, rows_here),
        labels.reshape(1, rows_here),
        embeddings,
        out=shape(PEERS, cap + PEERS, width, dtype=bf16),
    )
    got = exchange(sent, "plant")
    rows, tags, part = call(
        functools.partial(take_rows, cap),
        got,
        weights,
        out=(shape(slots, width, dtype=bf16), shape(PEERS, slots), shape(PEERS, slots)),
    )
    got = exchange(part, "feat")
    curv, part = call(
        to_residual, got, tags, rows, out=(shape(PEERS, slots), shape(PEERS, width + LANES))
    )
    got = exchange(part, "samp")
    grad, count, part = call(
        to_direction,
        got,
        weights,
        rows,
        out=(shape(1, width), shape(1, LANES), shape(PEERS, slots + LANES)),
    )
    got = exchange(part, "feat")
    proj, part = call(
        to_image, got, curv, rows, out=(shape(1, slots + LANES), shape(PEERS, width + LANES))
    )
    got = exchange(part, "samp")
    kept, part = call(
        to_second,
        got,
        proj,
        grad,
        count,
        rows,
        out=(shape(1, width + LANES), shape(PEERS, slots + 2 * LANES)),
    )
    got = exchange(part, "feat")
    scalars, part = call(
        to_bend, got, proj, curv, out=(shape(PEERS, LANES), shape(PEERS, LANES))
    )
    got = exchange(part, "samp")
    grad_share = lax.dynamic_slice_in_dim(grad, at, share, 1)
    resid_share = lax.dynamic_slice_in_dim(kept, at, share, 1)
    newton_step = call(
        to_step,
        got,
        count,
        scalars,
        kept[:, width:],
        grad_share,
        resid_share,
        out=shape(1, share),
    )
    return newton_step, grad_share


def solution(mesh):
    placed = (
        P(("plant", "samp"), "feat"),
        P(("plant", "samp"), None),
        P(("plant", "samp")),
        P("plant", "feat"),
    )
    return jax.shard_map(
        shards,
        mesh=mesh,
        in_specs=placed,
        out_specs=(P("plant", ("feat", "samp")), P("plant", ("feat", "samp"))),
        check_vma=False,
    )
```

```python
import functools

import jax
import jax.numpy as jnp
from jax import lax
from jax.experimental import pallas as pl
from jax.experimental.pallas import tpu as pltpu
from jax.sharding import PartitionSpec as P

penalty = 0.1
PEERS = 8
LANES = 128
GRANT = 12 << 20
f32 = jnp.float32
bf16 = jnp.bfloat16


def nt(a, b):
    return lax.dot_general(a, b, (((1,), (1,)), ((), ())), preferred_element_type=f32)


def nn(a, b):
    return lax.dot_general(a, b, (((1,), (0,)), ((), ())), preferred_element_type=f32)


def rep(row):
    return jnp.broadcast_to(row, (PEERS, row.shape[1]))


def total_of(ref):
    parts = [ref[p] for p in range(PEERS)]
    while len(parts) > 1:
        parts = [a + b for a, b in zip(parts[::2], parts[1::2])]
    return parts[0]


def send(ref, *rows):
    at = 0
    for row in rows:
        for p in range(PEERS):
            ref[p, :, at : at + row.shape[1]] = row
        at = at + row.shape[1]


def lanes(scalar):
    return jnp.broadcast_to(scalar, (1, LANES))


def row_sum(row):
    return jnp.sum(row, axis=1, keepdims=True)


def call(kernel, *args, out):
    return pl.pallas_call(
        kernel,
        out_shape=out,
        in_specs=[pl.BlockSpec(memory_space=pltpu.VMEM)] * len(args),
        out_specs=jax.tree.map(lambda _: pl.BlockSpec(memory_space=pltpu.VMEM), out),
        compiler_params=pltpu.CompilerParams(vmem_limit_bytes=GRANT),
        name=kernel.func.__name__ if isinstance(kernel, functools.partial) else kernel.__name__,
    )(*args)


def shape(*dims, dtype=f32):
    return jax.ShapeDtypeStruct(dims, dtype)


def pack_rows(cap, ids_ref, lab_ref, emb_ref, out_ref):
    rows = emb_ref.shape[0]
    ids = ids_ref[...]
    heads = lax.broadcasted_iota(jnp.int32, (PEERS, rows), 0)
    members = heads == ids
    mem_f = members.astype(f32)
    earlier = lax.broadcasted_iota(jnp.int32, (rows, rows), 0) < lax.broadcasted_iota(
        jnp.int32, (rows, rows), 1
    )
    before = nn(mem_f.astype(bf16), earlier.astype(f32).astype(bf16))
    rank = jnp.sum(before * mem_f, axis=0, keepdims=True).astype(jnp.int32)
    at_rank = lax.broadcasted_iota(jnp.int32, (cap, rows), 0) == rank
    tags = (lab_ref[...] + 1).astype(f32)
    tag_slots = nt((mem_f * tags).astype(bf16), at_rank.astype(f32).astype(bf16))
    emb = emb_ref[...]
    for p in range(PEERS):
        pick = (at_rank & (ids == p)).astype(f32).astype(bf16)
        out_ref[p, :cap, :] = nn(pick, emb).astype(bf16)
        out_ref[p, cap:, :cap] = jnp.broadcast_to(tag_slots[p : p + 1], (PEERS, cap)).astype(bf16)
        out_ref[p, cap:, cap:] = jnp.zeros((PEERS, rows - cap), bf16)


def take_rows(cap, got_ref, w_ref, rows_ref, tags_ref, out_ref):
    for p in range(PEERS):
        rows_ref[p * cap : (p + 1) * cap, :] = got_ref[p, :cap, :]
        tags_ref[:, p * cap : (p + 1) * cap] = got_ref[p, cap:, :cap].astype(f32)[:1]
    send(out_ref, nt(rep(w_ref[...]).astype(bf16), rows_ref[...])[:1])


def to_residual(got_ref, tags_ref, rows_ref, curv_ref, out_ref):
    logits = total_of(got_ref)
    tags = tags_ref[...]
    valid = tags > 0.0
    prob = jax.nn.sigmoid(logits)
    residual = jnp.where(valid, prob - jnp.maximum(tags - 1.0, 0.0), 0.0)
    curv_ref[...] = jnp.where(valid, prob * (1.0 - prob), 0.0)
    part = nn(rep(residual).astype(bf16), rows_ref[...])[:1]
    send(out_ref, part, lanes(row_sum(valid.astype(f32))))


def to_direction(got_ref, w_ref, rows_ref, grad_ref, count_ref, out_ref):
    width = rows_ref.shape[1]
    total = total_of(got_ref)
    count = total[:, width : width + 1]
    grad = total[:, :width] / count + penalty * w_ref[...]
    grad_ref[...] = grad
    count_ref[...] = lanes(count)
    part = nt(rep(-grad).astype(bf16), rows_ref[...])[:1]
    send(out_ref, part, lanes(row_sum(grad * grad)))


def to_image(got_ref, curv_ref, rows_ref, proj_ref, out_ref):
    slots = rows_ref.shape[0]
    total = total_of(got_ref)
    proj_ref[...] = total
    proj = total[:, :slots]
    weighted = (curv_ref[...] * proj).astype(bf16).astype(f32)
    part = nn(rep(weighted).astype(bf16), rows_ref[...])[:1]
    send(out_ref, part, lanes(row_sum(weighted * proj)))


def to_second(got_ref, proj_ref, grad_ref, count_ref, rows_ref, resid_ref, step_ref, out_ref):
    width, slots = rows_ref.shape[1], rows_ref.shape[0]
    total = total_of(got_ref)
    count = count_ref[:, :1]
    sq_norm = proj_ref[:, slots : slots + 1]
    direction = -grad_ref[...]
    image = total[:, :width] / count + penalty * direction
    step = sq_norm / (total[:, width : width + 1] / count + penalty * sq_norm)
    resid = direction - step * image
    resid_ref[...] = resid
    step_ref[...] = lanes(step)
    part = nt(rep(resid).astype(bf16), rows_ref[...])[:1]
    send(out_ref, part, lanes(row_sum(resid * resid)), lanes(row_sum(resid * direction)))


def to_bend(got_ref, proj_ref, curv_ref, keep_ref, out_ref):
    slots = curv_ref.shape[1]
    total = total_of(got_ref)
    sq_norm = proj_ref[:, slots : slots + 1]
    sq_next = total[:, slots : slots + 1]
    cross = total[:, slots + LANES : slots + LANES + 1]
    beta = sq_next / sq_norm
    proj = total[:, :slots] + beta * proj_ref[:, :slots]
    weighted = (curv_ref[...] * proj).astype(bf16).astype(f32)
    send(out_ref, lanes(row_sum(weighted * proj)))
    dir_sq = sq_next + 2.0 * beta * cross + beta * beta * sq_norm
    keep_ref[:, :LANES] = lanes(beta)
    keep_ref[:, LANES : 2 * LANES] = lanes(sq_next)
    keep_ref[:, 2 * LANES :] = lanes(dir_sq)


def to_step(got_ref, count_ref, keep_ref, first_ref, grad_ref, resid_ref, out_ref):
    beta = keep_ref[:, :1]
    sq_next = keep_ref[:, LANES : LANES + 1]
    dir_sq = keep_ref[:, 2 * LANES : 2 * LANES + 1]
    bend = total_of(got_ref)[:, :1]
    step = sq_next / (bend / count_ref[:, :1] + penalty * dir_sq)
    direction = -grad_ref[...]
    out_ref[...] = first_ref[:, :1] * direction + step * (resid_ref[...] + beta * direction)


def exchange(values, axis):
    return lax.all_to_all(values, axis, split_axis=0, concat_axis=0, tiled=True)


def shards(embeddings, plant_ids, labels, weights):
    rows_here, width = embeddings.shape
    samps = lax.axis_size("samp")
    share = width // samps
    cap = 2 * rows_here // PEERS
    slots = PEERS * cap
    at = lax.axis_index("samp") * share

    sent = call(
        functools.partial(pack_rows, cap),
        plant_ids.reshape(1, rows_here),
        labels.reshape(1, rows_here),
        embeddings,
        out=shape(PEERS, cap + PEERS, width, dtype=bf16),
    )
    got = exchange(sent, "plant")
    rows, tags, part = call(
        functools.partial(take_rows, cap),
        got,
        weights,
        out=(shape(slots, width, dtype=bf16), shape(1, slots), shape(PEERS, 1, slots)),
    )
    got = exchange(part, "feat")
    curv, part = call(
        to_residual, got, tags, rows, out=(shape(1, slots), shape(PEERS, 1, width + LANES))
    )
    got = exchange(part, "samp")
    grad, count, part = call(
        to_direction,
        got,
        weights,
        rows,
        out=(shape(1, width), shape(1, LANES), shape(PEERS, 1, slots + LANES)),
    )
    got = exchange(part, "feat")
    proj, part = call(
        to_image, got, curv, rows, out=(shape(1, slots + LANES), shape(PEERS, 1, width + LANES))
    )
    got = exchange(part, "samp")
    resid, first, part = call(
        to_second,
        got,
        proj,
        grad,
        count,
        rows,
        out=(shape(1, width), shape(1, LANES), shape(PEERS, 1, slots + 2 * LANES)),
    )
    got = exchange(part, "feat")
    scalars, part = call(
        to_bend, got, proj, curv, out=(shape(1, 3 * LANES), shape(PEERS, 1, LANES))
    )
    got = exchange(part, "samp")
    grad_share = lax.dynamic_slice_in_dim(grad, at, share, 1)
    resid_share = lax.dynamic_slice_in_dim(resid, at, share, 1)
    newton_step = call(
        to_step,
        got,
        count,
        scalars,
        first,
        grad_share,
        resid_share,
        out=shape(1, share),
    )
    return newton_step, grad_share


def solution(mesh):
    placed = (
        P(("plant", "samp"), "feat"),
        P(("plant", "samp"), None),
        P(("plant", "samp")),
        P("plant", "feat"),
    )
    return jax.shard_map(
        shards,
        mesh=mesh,
        in_specs=placed,
        out_specs=(P("plant", ("feat", "samp")), P("plant", ("feat", "samp"))),
        check_vma=False,
    )
```

```python
import functools

import jax
import jax.numpy as jnp
from jax import lax
from jax.experimental import pallas as pl
from jax.experimental.pallas import tpu as pltpu
from jax.sharding import PartitionSpec as P

penalty = 0.1
PEERS = 8
LANES = 128
GRANT = 12 << 20
f32 = jnp.float32
bf16 = jnp.bfloat16


def nt(a, b):
    return lax.dot_general(a, b, (((1,), (1,)), ((), ())), preferred_element_type=f32)


def nn(a, b):
    return lax.dot_general(a, b, (((1,), (0,)), ((), ())), preferred_element_type=f32)


def rep(row):
    return jnp.broadcast_to(row, (PEERS, row.shape[1]))


def total_of(ref):
    parts = [ref[p] for p in range(PEERS)]
    while len(parts) > 1:
        parts = [a + b for a, b in zip(parts[::2], parts[1::2])]
    return parts[0]


def send(ref, *rows):
    at = 0
    for row in rows:
        for p in range(PEERS):
            ref[p, :, at : at + row.shape[1]] = row
        at = at + row.shape[1]


def lanes(scalar):
    return jnp.broadcast_to(scalar, (1, LANES))


def row_sum(row):
    return jnp.sum(row, axis=1, keepdims=True)


def call(kernel, *args, out, scratch=(), space=pltpu.VMEM):
    return pl.pallas_call(
        kernel,
        out_shape=out,
        in_specs=[pl.BlockSpec(memory_space=space)] * len(args),
        scratch_shapes=scratch,
        out_specs=jax.tree.map(lambda _: pl.BlockSpec(memory_space=pltpu.VMEM), out),
        compiler_params=pltpu.CompilerParams(vmem_limit_bytes=GRANT),
        name=kernel.func.__name__ if isinstance(kernel, functools.partial) else kernel.__name__,
    )(*args)


def shape(*dims, dtype=f32):
    return jax.ShapeDtypeStruct(dims, dtype)


def pack_rows(cap, ids_in, lab_in, emb_in, out_ref, ids_ref, lab_ref, emb_ref, sems):
    copies = [
        pltpu.make_async_copy(src, dst, sems.at[k])
        for k, (src, dst) in enumerate(
            ((ids_in, ids_ref), (lab_in, lab_ref), (emb_in, emb_ref))
        )
    ]
    for copy in copies:
        copy.start()
    rows = emb_ref.shape[0]
    heads = lax.broadcasted_iota(jnp.int32, (PEERS, rows), 0)
    earlier = lax.broadcasted_iota(jnp.int32, (rows, rows), 0) < lax.broadcasted_iota(
        jnp.int32, (rows, rows), 1
    )
    earlier = earlier.astype(f32).astype(bf16)
    copies[0].wait()
    copies[1].wait()
    ids = ids_ref[...]
    mem_f = (heads == ids).astype(f32)
    before = nn(mem_f.astype(bf16), earlier)
    rank = jnp.sum(before * mem_f, axis=0, keepdims=True).astype(jnp.int32)
    at_rank = lax.broadcasted_iota(jnp.int32, (cap, rows), 0) == rank
    tags = (lab_ref[...] + 1).astype(f32)
    tag_slots = nt((mem_f * tags).astype(bf16), at_rank.astype(f32).astype(bf16))
    copies[2].wait()
    emb = emb_ref[...]
    for p in range(PEERS):
        pick = (at_rank & (ids == p)).astype(f32).astype(bf16)
        out_ref[p, :cap, :] = nn(pick, emb).astype(bf16)
        out_ref[p, cap:, :cap] = jnp.broadcast_to(tag_slots[p : p + 1], (PEERS, cap)).astype(bf16)
        out_ref[p, cap:, cap:] = jnp.zeros((PEERS, rows - cap), bf16)


def take_rows(cap, got_ref, w_ref, rows_ref, tags_ref, out_ref):
    for p in range(PEERS):
        rows_ref[p * cap : (p + 1) * cap, :] = got_ref[p, :cap, :]
        tags_ref[:, p * cap : (p + 1) * cap] = got_ref[p, cap:, :cap].astype(f32)[:1]
    send(out_ref, nt(rep(w_ref[...]).astype(bf16), rows_ref[...])[:1])


def to_residual(got_ref, tags_ref, rows_ref, curv_ref, out_ref):
    logits = total_of(got_ref)
    tags = tags_ref[...]
    valid = tags > 0.0
    prob = jax.nn.sigmoid(logits)
    residual = jnp.where(valid, prob - jnp.maximum(tags - 1.0, 0.0), 0.0)
    curv_ref[...] = jnp.where(valid, prob * (1.0 - prob), 0.0)
    part = nn(rep(residual).astype(bf16), rows_ref[...])[:1]
    send(out_ref, part, lanes(row_sum(valid.astype(f32))))


def to_direction(got_ref, w_ref, rows_ref, grad_ref, count_ref, out_ref):
    width = rows_ref.shape[1]
    total = total_of(got_ref)
    count = total[:, width : width + 1]
    grad = total[:, :width] / count + penalty * w_ref[...]
    grad_ref[...] = grad
    count_ref[...] = lanes(count)
    part = nt(rep(-grad).astype(bf16), rows_ref[...])[:1]
    send(out_ref, part, lanes(row_sum(grad * grad)))


def to_image(got_ref, curv_ref, rows_ref, sq_norm_ref, out_ref):
    slots = rows_ref.shape[0]
    total = total_of(got_ref)
    sq_norm_ref[...] = total[:, slots:]
    proj = total[:, :slots]
    curv = curv_ref[...]
    weighted = (curv * proj).astype(bf16).astype(f32)
    part = nn(rep(weighted).astype(bf16), rows_ref[...])[:1]
    send(out_ref, part, lanes(row_sum(weighted * proj)), jnp.sqrt(curv) * proj)


def to_second(got_ref, sq_norm_ref, curv_ref, grad_ref, count_ref, rows_ref, resid_ref, step_ref, out_ref):
    width, cap = rows_ref.shape[1], rows_ref.shape[0] // PEERS
    total = got_ref[0, :, : width + LANES]
    for p in range(1, PEERS):
        total = total + got_ref[p, :, : width + LANES]
    count = count_ref[:, :1]
    sq_norm = sq_norm_ref[:, :1]
    direction = -grad_ref[...]
    image = total[:, :width] / count + penalty * direction
    step = sq_norm / (total[:, width : width + 1] / count + penalty * sq_norm)
    resid = direction - step * image
    resid_ref[...] = resid
    step_ref[...] = lanes(step)
    part = nt(rep(resid).astype(bf16), rows_ref[...]) * jnp.sqrt(curv_ref[...])
    source = lax.broadcasted_iota(jnp.int32, (PEERS, cap), 0)
    tile = part[:, :cap]
    for p in range(1, PEERS):
        tile = jnp.where(source == p, part[:, p * cap : (p + 1) * cap], tile)
    tile = tile.astype(bf16)
    for peer in range(out_ref.shape[0]):
        out_ref[peer] = tile


def to_tiles(got_ref, out_ref):
    groups, cap = out_ref.shape[0], out_ref.shape[2]
    start = got_ref.shape[2] - PEERS * cap
    for s in range(groups):
        for p in range(PEERS):
            out_ref[s, p : p + 1, :] = got_ref[s, :, start + p * cap : start + (p + 1) * cap]


def to_step(got_ref, first_ref, count_ref, sq_norm_ref, step_ref, grad_ref, resid_ref, out_ref):
    groups = first_ref.shape[0]
    feats = got_ref.shape[0] // groups
    first_sq, cross, second_sq = 0.0, 0.0, 0.0
    for s in range(groups):
        first = first_ref[s]
        second = got_ref[s].astype(f32)
        for f in range(1, feats):
            second = second + got_ref[f * groups + s].astype(f32)
        first_sq = first_sq + first * first
        cross = cross + first * second
        second_sq = second_sq + second * second
    first_sq, cross, second_sq = (
        jnp.sum(row_sum(v), axis=0, keepdims=True) for v in (first_sq, cross, second_sq)
    )
    count, sq_norm, first_step = count_ref[:, :1], sq_norm_ref[:, :1], step_ref[:, :1]
    sq_next = -first_step * cross / count
    beta = sq_next / sq_norm
    bend = second_sq + 2.0 * beta * cross + beta * beta * first_sq
    step = sq_next / (bend / count + penalty * (sq_next + beta * beta * sq_norm))
    direction = -grad_ref[...]
    out_ref[...] = first_step * direction + step * (resid_ref[...] + beta * direction)


def exchange(values, axis):
    return lax.all_to_all(values, axis, split_axis=0, concat_axis=0, tiled=True)


def shards(embeddings, plant_ids, labels, weights):
    rows_here, width = embeddings.shape
    samps = lax.axis_size("samp")
    share = width // samps
    cap = 2 * rows_here // PEERS
    slots = PEERS * cap
    at = lax.axis_index("samp") * share

    sent = call(
        functools.partial(pack_rows, cap),
        *(
            pltpu.with_memory_space_constraint(v, pltpu.HBM)
            for v in (plant_ids.reshape(1, rows_here), labels.reshape(1, rows_here), embeddings)
        ),
        out=shape(PEERS, cap + PEERS, width, dtype=bf16),
        scratch=(
            pltpu.VMEM((1, rows_here), jnp.int32),
            pltpu.VMEM((1, rows_here), jnp.int32),
            pltpu.VMEM((rows_here, width), bf16),
            pltpu.SemaphoreType.DMA((3,)),
        ),
        space=pltpu.HBM,
    )
    got = exchange(sent, "plant")
    rows, tags, part = call(
        functools.partial(take_rows, cap),
        got,
        weights,
        out=(shape(slots, width, dtype=bf16), shape(1, slots), shape(PEERS, 1, slots)),
    )
    got = exchange(part, "feat")
    curv, part = call(
        to_residual, got, tags, rows, out=(shape(1, slots), shape(PEERS, 1, width + LANES))
    )
    got = exchange(part, "samp")
    grad, count, part = call(
        to_direction,
        got,
        weights,
        rows,
        out=(shape(1, width), shape(1, LANES), shape(PEERS, 1, slots + LANES)),
    )
    got = exchange(part, "feat")
    sq_norm, part = call(
        to_image,
        got,
        curv,
        rows,
        out=(shape(1, LANES), shape(PEERS, 1, width + LANES + slots)),
    )
    got = exchange(part, "samp")
    resid, first_step, part = call(
        to_second,
        got,
        sq_norm,
        curv,
        grad,
        count,
        rows,
        out=(
            shape(1, width),
            shape(1, LANES),
            shape(lax.axis_size("feat") * samps, PEERS, cap, dtype=bf16),
        ),
    )
    first = call(to_tiles, got, out=shape(samps, PEERS, cap))
    got = exchange(part, ("feat", "samp"))
    grad_share = lax.dynamic_slice_in_dim(grad, at, share, 1)
    resid_share = lax.dynamic_slice_in_dim(resid, at, share, 1)
    newton_step = call(
        to_step,
        got,
        first,
        count,
        sq_norm,
        first_step,
        grad_share,
        resid_share,
        out=shape(1, share),
    )
    return newton_step, grad_share


def solution(mesh):
    placed = (
        P(("plant", "samp"), "feat"),
        P(("plant", "samp"), None),
        P(("plant", "samp")),
        P("plant", "feat"),
    )
    return jax.shard_map(
        shards,
        mesh=mesh,
        in_specs=placed,
        out_specs=(P("plant", ("feat", "samp")), P("plant", ("feat", "samp"))),
        check_vma=False,
    )
```

```python
import functools

import jax
import jax.numpy as jnp
from jax import lax
from jax.experimental import pallas as pl
from jax.experimental.pallas import tpu as pltpu
from jax.sharding import PartitionSpec as P

penalty = 0.1
PEERS = 8
LANES = 128
GRANT = 12 << 20
f32 = jnp.float32
bf16 = jnp.bfloat16


def nt(a, b):
    return lax.dot_general(a, b, (((1,), (1,)), ((), ())), preferred_element_type=f32)


def nn(a, b):
    return lax.dot_general(a, b, (((1,), (0,)), ((), ())), preferred_element_type=f32)


def rep(row):
    return jnp.broadcast_to(row, (PEERS, row.shape[1]))


def total_of(ref):
    parts = [ref[p] for p in range(PEERS)]
    while len(parts) > 1:
        parts = [a + b for a, b in zip(parts[::2], parts[1::2])]
    return parts[0]


def send(ref, *rows):
    at = 0
    for row in rows:
        for p in range(PEERS):
            ref[p, :, at : at + row.shape[1]] = row
        at = at + row.shape[1]


def lanes(scalar):
    return jnp.broadcast_to(scalar, (1, LANES))


def row_sum(row):
    return jnp.sum(row, axis=1, keepdims=True)


def call(kernel, *args, out, scratch=(), space=pltpu.VMEM):
    return pl.pallas_call(
        kernel,
        out_shape=out,
        in_specs=[pl.BlockSpec(memory_space=space)] * len(args),
        scratch_shapes=scratch,
        out_specs=jax.tree.map(lambda _: pl.BlockSpec(memory_space=pltpu.VMEM), out),
        compiler_params=pltpu.CompilerParams(vmem_limit_bytes=GRANT),
        name=kernel.func.__name__ if isinstance(kernel, functools.partial) else kernel.__name__,
    )(*args)


def shape(*dims, dtype=f32):
    return jax.ShapeDtypeStruct(dims, dtype)


def pack_rows(cap, ids_in, lab_in, emb_in, out_ref, ids_ref, lab_ref, emb_ref, sems):
    copies = [
        pltpu.make_async_copy(src, dst, sems.at[k])
        for k, (src, dst) in enumerate(
            ((ids_in, ids_ref), (lab_in, lab_ref), (emb_in, emb_ref))
        )
    ]
    for copy in copies:
        copy.start()
    rows = emb_ref.shape[0]
    heads = lax.broadcasted_iota(jnp.int32, (PEERS, rows), 0)
    earlier = lax.broadcasted_iota(jnp.int32, (rows, rows), 0) < lax.broadcasted_iota(
        jnp.int32, (rows, rows), 1
    )
    earlier = earlier.astype(f32).astype(bf16)
    copies[0].wait()
    copies[1].wait()
    ids = ids_ref[...]
    mem_f = (heads == ids).astype(f32)
    before = nn(mem_f.astype(bf16), earlier)
    rank = jnp.sum(before * mem_f, axis=0, keepdims=True).astype(jnp.int32)
    at_rank = lax.broadcasted_iota(jnp.int32, (cap, rows), 0) == rank
    tags = (lab_ref[...] + 1).astype(f32)
    tag_slots = nt((mem_f * tags).astype(bf16), at_rank.astype(f32).astype(bf16))
    copies[2].wait()
    emb = emb_ref[...]
    for p in range(PEERS):
        pick = (at_rank & (ids == p)).astype(f32).astype(bf16)
        out_ref[p, :cap, :] = nn(pick, emb).astype(bf16)
        out_ref[p, cap:, :cap] = jnp.broadcast_to(tag_slots[p : p + 1], (PEERS, cap)).astype(bf16)
        out_ref[p, cap:, cap:] = jnp.zeros((PEERS, rows - cap), bf16)


def take_rows(cap, got_ref, w_ref, rows_ref, tags_ref, out_ref):
    for p in range(PEERS):
        rows_ref[p * cap : (p + 1) * cap, :] = got_ref[p, :cap, :]
        tags_ref[:, p * cap : (p + 1) * cap] = got_ref[p, cap:, :cap].astype(f32)[:1]
    send(out_ref, nt(rep(w_ref[...]).astype(bf16), rows_ref[...])[:1])


def to_residual(got_ref, tags_ref, rows_ref, curv_ref, out_ref):
    logits = total_of(got_ref)
    tags = tags_ref[...]
    valid = tags > 0.0
    prob = jax.nn.sigmoid(logits)
    residual = jnp.where(valid, prob - jnp.maximum(tags - 1.0, 0.0), 0.0)
    curv_ref[...] = jnp.where(valid, prob * (1.0 - prob), 0.0)
    part = nn(rep(residual).astype(bf16), rows_ref[...])[:1]
    send(out_ref, part, lanes(row_sum(valid.astype(f32))))


def own_share(row, share):
    width = row.shape[1]
    at = lax.axis_index("samp") * share
    return pltpu.roll(row, lax.rem(width - at, width), 1)[:, :share]


def to_direction(got_ref, w_ref, rows_ref, grad_ref, count_ref, share_ref, out_ref):
    width = rows_ref.shape[1]
    total = total_of(got_ref)
    count = total[:, width : width + 1]
    grad = total[:, :width] / count + penalty * w_ref[...]
    grad_ref[...] = grad
    count_ref[...] = lanes(count)
    share_ref[...] = own_share(grad, share_ref.shape[1])
    part = nt(rep(-grad).astype(bf16), rows_ref[...])[:1]
    send(out_ref, part, lanes(row_sum(grad * grad)))


def to_image(got_ref, curv_ref, rows_ref, proj_ref, out_ref):
    slots = rows_ref.shape[0]
    total = total_of(got_ref)
    proj_ref[...] = total
    proj = total[:, :slots]
    weighted = (curv_ref[...] * proj).astype(bf16).astype(f32)
    part = nn(rep(weighted).astype(bf16), rows_ref[...])[:1]
    send(out_ref, part, lanes(row_sum(weighted * proj)))


def to_second(got_ref, proj_ref, grad_ref, count_ref, rows_ref, keep_ref, out_ref):
    width, slots = rows_ref.shape[1], rows_ref.shape[0]
    total = total_of(got_ref)
    count = count_ref[:, :1]
    sq_norm = proj_ref[:, slots : slots + 1]
    direction = -grad_ref[...]
    image = total[:, :width] / count + penalty * direction
    step = sq_norm / (total[:, width : width + 1] / count + penalty * sq_norm)
    resid = direction - step * image
    share = keep_ref.shape[1] - LANES
    keep_ref[:, :LANES] = lanes(step)
    keep_ref[:, LANES:] = own_share(resid, share)
    part = nt(rep(resid).astype(bf16), rows_ref[...])[:1]
    send(out_ref, part, lanes(row_sum(resid * resid)), lanes(row_sum(resid * direction)))


def to_bend(got_ref, proj_ref, curv_ref, keep_ref, out_ref):
    slots = curv_ref.shape[1]
    total = total_of(got_ref)
    sq_norm = proj_ref[:, slots : slots + 1]
    sq_next = total[:, slots : slots + 1]
    cross = total[:, slots + LANES : slots + LANES + 1]
    beta = sq_next / sq_norm
    proj = total[:, :slots] + beta * proj_ref[:, :slots]
    weighted = (curv_ref[...] * proj).astype(bf16).astype(f32)
    send(out_ref, lanes(row_sum(weighted * proj)))
    dir_sq = sq_next + 2.0 * beta * cross + beta * beta * sq_norm
    keep_ref[:, :LANES] = lanes(beta)
    keep_ref[:, LANES : 2 * LANES] = lanes(sq_next)
    keep_ref[:, 2 * LANES :] = lanes(dir_sq)


def to_step(got_ref, count_ref, scalars_ref, first_ref, grad_ref, out_ref):
    beta = scalars_ref[:, :1]
    sq_next = scalars_ref[:, LANES : LANES + 1]
    dir_sq = scalars_ref[:, 2 * LANES : 2 * LANES + 1]
    bend = total_of(got_ref)[:, :1]
    step = sq_next / (bend / count_ref[:, :1] + penalty * dir_sq)
    direction = -grad_ref[...]
    resid = first_ref[:, LANES:]
    out_ref[...] = first_ref[:, :1] * direction + step * (resid + beta * direction)


def exchange(values, axis):
    return lax.all_to_all(values, axis, split_axis=0, concat_axis=0, tiled=True)


def shards(embeddings, plant_ids, labels, weights):
    rows_here, width = embeddings.shape
    samps = lax.axis_size("samp")
    share = width // samps
    cap = 2 * rows_here // PEERS
    slots = PEERS * cap

    sent = call(
        functools.partial(pack_rows, cap),
        *(
            pltpu.with_memory_space_constraint(v, pltpu.HBM)
            for v in (plant_ids.reshape(1, rows_here), labels.reshape(1, rows_here), embeddings)
        ),
        out=shape(PEERS, cap + PEERS, width, dtype=bf16),
        scratch=(
            pltpu.VMEM((1, rows_here), jnp.int32),
            pltpu.VMEM((1, rows_here), jnp.int32),
            pltpu.VMEM((rows_here, width), bf16),
            pltpu.SemaphoreType.DMA((3,)),
        ),
        space=pltpu.HBM,
    )
    got = exchange(sent, "plant")
    rows, tags, part = call(
        functools.partial(take_rows, cap),
        got,
        weights,
        out=(shape(slots, width, dtype=bf16), shape(1, slots), shape(PEERS, 1, slots)),
    )
    got = exchange(part, "feat")
    curv, part = call(
        to_residual, got, tags, rows, out=(shape(1, slots), shape(PEERS, 1, width + LANES))
    )
    got = exchange(part, "samp")
    grad, count, grad_share, part = call(
        to_direction,
        got,
        weights,
        rows,
        out=(
            shape(1, width),
            shape(1, LANES),
            shape(1, share),
            shape(PEERS, 1, slots + LANES),
        ),
    )
    got = exchange(part, "feat")
    proj, part = call(
        to_image, got, curv, rows, out=(shape(1, slots + LANES), shape(PEERS, 1, width + LANES))
    )
    got = exchange(part, "samp")
    first, part = call(
        to_second,
        got,
        proj,
        grad,
        count,
        rows,
        out=(shape(1, LANES + share), shape(PEERS, 1, slots + 2 * LANES)),
    )
    got = exchange(part, "feat")
    scalars, part = call(
        to_bend, got, proj, curv, out=(shape(1, 3 * LANES), shape(PEERS, 1, LANES))
    )
    got = exchange(part, "samp")
    newton_step = call(
        to_step, got, count, scalars, first, grad_share, out=shape(1, share)
    )
    return newton_step, grad_share


def solution(mesh):
    placed = (
        P(("plant", "samp"), "feat"),
        P(("plant", "samp"), None),
        P(("plant", "samp")),
        P("plant", "feat"),
    )
    return jax.shard_map(
        shards,
        mesh=mesh,
        in_specs=placed,
        out_specs=(P("plant", ("feat", "samp")), P("plant", ("feat", "samp"))),
        check_vma=False,
    )
```

```python
import functools

import jax
import jax.numpy as jnp
from jax import lax
from jax.experimental import pallas as pl
from jax.experimental.pallas import tpu as pltpu
from jax.sharding import PartitionSpec as P

penalty = 0.1
PEERS = 8
LANES = 128
DEEP = 16
GRANT = 12 << 20
f32 = jnp.float32
bf16 = jnp.bfloat16


def nt(a, b):
    return lax.dot_general(a, b, (((1,), (1,)), ((), ())), preferred_element_type=f32)


def nn(a, b):
    return lax.dot_general(a, b, (((1,), (0,)), ((), ())), preferred_element_type=f32)


def rep(row):
    return jnp.broadcast_to(row, (PEERS, row.shape[1]))


def total_of(ref):
    parts = [ref[p] for p in range(PEERS)]
    while len(parts) > 1:
        parts = [a + b for a, b in zip(parts[::2], parts[1::2])]
    return parts[0]


def send(ref, *rows):
    at = 0
    for row in rows:
        for p in range(PEERS):
            ref[p, :, at : at + row.shape[1]] = row
        at = at + row.shape[1]


def lanes(scalar):
    return jnp.broadcast_to(scalar, (1, LANES))


def row_sum(row):
    return jnp.sum(row, axis=1, keepdims=True)


def call(kernel, *args, out, scratch=(), space=pltpu.VMEM):
    return pl.pallas_call(
        kernel,
        out_shape=out,
        in_specs=[pl.BlockSpec(memory_space=space)] * len(args),
        scratch_shapes=scratch,
        out_specs=jax.tree.map(lambda _: pl.BlockSpec(memory_space=pltpu.VMEM), out),
        compiler_params=pltpu.CompilerParams(vmem_limit_bytes=GRANT),
        name=kernel.func.__name__ if isinstance(kernel, functools.partial) else kernel.__name__,
    )(*args)


def shape(*dims, dtype=f32):
    return jax.ShapeDtypeStruct(dims, dtype)


def pack_rows(cap, ids_in, lab_in, emb_in, out_ref, ids_ref, lab_ref, emb_ref, sems):
    copies = [
        pltpu.make_async_copy(src, dst, sems.at[k])
        for k, (src, dst) in enumerate(
            ((ids_in, ids_ref), (lab_in, lab_ref), (emb_in, emb_ref))
        )
    ]
    for copy in copies:
        copy.start()
    rows = emb_ref.shape[0]
    heads = lax.broadcasted_iota(jnp.int32, (PEERS, rows), 0)
    earlier = lax.broadcasted_iota(jnp.int32, (rows, rows), 0) < lax.broadcasted_iota(
        jnp.int32, (rows, rows), 1
    )
    earlier = earlier.astype(f32).astype(bf16)
    copies[0].wait()
    copies[1].wait()
    ids = ids_ref[...]
    mem_f = (heads == ids).astype(f32)
    before = nn(mem_f.astype(bf16), earlier)
    rank = jnp.sum(before * mem_f, axis=0, keepdims=True).astype(jnp.int32)
    at_rank = lax.broadcasted_iota(jnp.int32, (cap, rows), 0) == rank
    tags = (lab_ref[...] + 1).astype(f32)
    tag_slots = nt((mem_f * tags).astype(bf16), at_rank.astype(f32).astype(bf16))
    copies[2].wait()
    emb = emb_ref[...]
    across = emb.shape[1] // LANES
    for p in range(PEERS):
        pick = (at_rank & (ids == p)).astype(f32).astype(bf16)
        picked = nn(pick, emb).astype(bf16)
        for down in range(cap // DEEP):
            for over in range(across):
                out_ref[p, down * across + over] = picked[
                    down * DEEP : (down + 1) * DEEP, over * LANES : (over + 1) * LANES
                ]
        out_ref[p, cap // DEEP * across] = jnp.broadcast_to(
            tag_slots[p : p + 1], (DEEP, cap)
        ).astype(bf16)


def take_rows(cap, got_ref, w_ref, rows_ref, tags_ref, out_ref):
    across = rows_ref.shape[1] // LANES
    for p in range(PEERS):
        for down in range(cap // DEEP):
            for over in range(across):
                at = p * cap + down * DEEP
                rows_ref[at : at + DEEP, over * LANES : (over + 1) * LANES] = got_ref[
                    p, down * across + over
                ]
        tags_ref[:, p * cap : (p + 1) * cap] = got_ref[p, cap // DEEP * across].astype(f32)[:1]
    send(out_ref, nt(rep(w_ref[...]).astype(bf16), rows_ref[...])[:1])


def to_residual(got_ref, tags_ref, rows_ref, curv_ref, out_ref):
    logits = total_of(got_ref)
    tags = tags_ref[...]
    valid = tags > 0.0
    prob = jax.nn.sigmoid(logits)
    residual = jnp.where(valid, prob - jnp.maximum(tags - 1.0, 0.0), 0.0)
    curv_ref[...] = jnp.where(valid, prob * (1.0 - prob), 0.0)
    part = nn(rep(residual).astype(bf16), rows_ref[...])[:1]
    send(out_ref, part, lanes(row_sum(valid.astype(f32))))


def own_share(row, share):
    width = row.shape[1]
    at = lax.axis_index("samp") * share
    return pltpu.roll(row, lax.rem(width - at, width), 1)[:, :share]


def to_direction(got_ref, w_ref, rows_ref, grad_ref, count_ref, share_ref, out_ref):
    width = rows_ref.shape[1]
    total = total_of(got_ref)
    count = total[:, width : width + 1]
    grad = total[:, :width] / count + penalty * w_ref[...]
    grad_ref[...] = grad
    count_ref[...] = lanes(count)
    share_ref[...] = own_share(grad, share_ref.shape[1])
    part = nt(rep(-grad).astype(bf16), rows_ref[...])[:1]
    send(out_ref, part, lanes(row_sum(grad * grad)))


def to_image(got_ref, curv_ref, rows_ref, sq_norm_ref, out_ref):
    slots = rows_ref.shape[0]
    total = total_of(got_ref)
    sq_norm_ref[...] = total[:, slots:]
    proj = total[:, :slots]
    curv = curv_ref[...]
    weighted = (curv * proj).astype(bf16).astype(f32)
    part = nn(rep(weighted).astype(bf16), rows_ref[...])[:1]
    send(out_ref, part, lanes(row_sum(weighted * proj)), jnp.sqrt(curv) * proj)


def to_second(got_ref, sq_norm_ref, curv_ref, grad_ref, count_ref, rows_ref, keep_ref, out_ref):
    width, cap = rows_ref.shape[1], rows_ref.shape[0] // PEERS
    total = got_ref[0, :, : width + LANES]
    for p in range(1, PEERS):
        total = total + got_ref[p, :, : width + LANES]
    count = count_ref[:, :1]
    sq_norm = sq_norm_ref[:, :1]
    direction = -grad_ref[...]
    image = total[:, :width] / count + penalty * direction
    step = sq_norm / (total[:, width : width + 1] / count + penalty * sq_norm)
    resid = direction - step * image
    keep_ref[:, :LANES] = lanes(step)
    keep_ref[:, LANES:] = own_share(resid, keep_ref.shape[1] - LANES)
    part = nt(rep(resid).astype(bf16), rows_ref[...]) * jnp.sqrt(curv_ref[...])
    source = lax.broadcasted_iota(jnp.int32, (PEERS, cap), 0)
    tile = part[:, :cap]
    for p in range(1, PEERS):
        tile = jnp.where(source == p, part[:, p * cap : (p + 1) * cap], tile)
    tile = tile.astype(bf16)
    for peer in range(out_ref.shape[0]):
        out_ref[peer] = tile


def to_step(got_ref, first_ref, count_ref, sq_norm_ref, keep_ref, share_ref, out_ref, grad_ref, tiles_ref):
    groups, _, cap = tiles_ref.shape
    feats = got_ref.shape[0] // groups
    start = first_ref.shape[2] - PEERS * cap
    for s in range(groups):
        for p in range(PEERS):
            tiles_ref[s, p : p + 1, :] = first_ref[s, :, start + p * cap : start + (p + 1) * cap]
    first_sq, cross, second_sq = 0.0, 0.0, 0.0
    for s in range(groups):
        first = tiles_ref[s]
        second = got_ref[s].astype(f32)
        for f in range(1, feats):
            second = second + got_ref[f * groups + s].astype(f32)
        first_sq = first_sq + first * first
        cross = cross + first * second
        second_sq = second_sq + second * second
    first_sq, cross, second_sq = (
        jnp.sum(row_sum(v), axis=0, keepdims=True) for v in (first_sq, cross, second_sq)
    )
    count, sq_norm, first_step = count_ref[:, :1], sq_norm_ref[:, :1], keep_ref[:, :1]
    sq_next = -first_step * cross / count
    beta = sq_next / sq_norm
    bend = second_sq + 2.0 * beta * cross + beta * beta * first_sq
    step = sq_next / (bend / count + penalty * (sq_next + beta * beta * sq_norm))
    grad_ref[...] = share_ref[...]
    direction = -share_ref[...]
    out_ref[...] = first_step * direction + step * (keep_ref[:, LANES:] + beta * direction)


def exchange(values, axis):
    return lax.all_to_all(values, axis, split_axis=0, concat_axis=0, tiled=True)


def shards(embeddings, plant_ids, labels, weights):
    rows_here, width = embeddings.shape
    samps = lax.axis_size("samp")
    share = width // samps
    cap = 2 * rows_here // PEERS
    slots = PEERS * cap

    sent = call(
        functools.partial(pack_rows, cap),
        *(
            pltpu.with_memory_space_constraint(v, pltpu.HBM)
            for v in (plant_ids.reshape(1, rows_here), labels.reshape(1, rows_here), embeddings)
        ),
        out=shape(PEERS, cap // DEEP * (width // LANES) + 1, DEEP, LANES, dtype=bf16),
        scratch=(
            pltpu.VMEM((1, rows_here), jnp.int32),
            pltpu.VMEM((1, rows_here), jnp.int32),
            pltpu.VMEM((rows_here, width), bf16),
            pltpu.SemaphoreType.DMA((3,)),
        ),
        space=pltpu.HBM,
    )
    got = exchange(sent, "plant")
    rows, tags, part = call(
        functools.partial(take_rows, cap),
        got,
        weights,
        out=(shape(slots, width, dtype=bf16), shape(1, slots), shape(PEERS, 1, slots)),
    )
    got = exchange(part, "feat")
    curv, part = call(
        to_residual, got, tags, rows, out=(shape(1, slots), shape(PEERS, 1, width + LANES))
    )
    got = exchange(part, "samp")
    grad, count, grad_share, part = call(
        to_direction,
        got,
        weights,
        rows,
        out=(
            shape(1, width),
            shape(1, LANES),
            shape(1, share),
            shape(PEERS, 1, slots + LANES),
        ),
    )
    got = exchange(part, "feat")
    sq_norm, first = call(
        to_image,
        got,
        curv,
        rows,
        out=(shape(1, LANES), shape(PEERS, 1, width + LANES + slots)),
    )
    first = exchange(first, "samp")
    keep, part = call(
        to_second,
        first,
        sq_norm,
        curv,
        grad,
        count,
        rows,
        out=(
            shape(1, LANES + share),
            shape(lax.axis_size("feat") * samps, PEERS, cap, dtype=bf16),
        ),
    )
    got = exchange(part, ("feat", "samp"))
    return call(
        to_step,
        got,
        first,
        count,
        sq_norm,
        keep,
        grad_share,
        out=(shape(1, share), shape(1, share)),
        scratch=(pltpu.VMEM((samps, PEERS, cap), f32),),
    )


def solution(mesh):
    placed = (
        P(("plant", "samp"), "feat"),
        P(("plant", "samp"), None),
        P(("plant", "samp")),
        P("plant", "feat"),
    )
    return jax.shard_map(
        shards,
        mesh=mesh,
        in_specs=placed,
        out_specs=(P("plant", ("feat", "samp")), P("plant", ("feat", "samp"))),
        check_vma=False,
    )
```

```python
import functools

import jax
import jax.numpy as jnp
from jax import lax
from jax.experimental import pallas as pl
from jax.experimental.pallas import tpu as pltpu
from jax.sharding import PartitionSpec as P

penalty = 0.1
PEERS = 8
LANES = 128
DEEP = 16
GRANT = 12 << 20
f32 = jnp.float32
bf16 = jnp.bfloat16


def nt(a, b):
    return lax.dot_general(a, b, (((1,), (1,)), ((), ())), preferred_element_type=f32)


def nn(a, b):
    return lax.dot_general(a, b, (((1,), (0,)), ((), ())), preferred_element_type=f32)


def rep(row):
    return jnp.broadcast_to(row, (PEERS, row.shape[1]))


def total_of(ref):
    parts = [ref[p] for p in range(PEERS)]
    while len(parts) > 1:
        parts = [a + b for a, b in zip(parts[::2], parts[1::2])]
    return parts[0]


def send(ref, *rows):
    at = 0
    for row in rows:
        for p in range(PEERS):
            ref[p, :, at : at + row.shape[1]] = row
        at = at + row.shape[1]


def lanes(scalar):
    return jnp.broadcast_to(scalar, (1, LANES))


def row_sum(row):
    return jnp.sum(row, axis=1, keepdims=True)


def call(kernel, *args, out, scratch=(), space=pltpu.VMEM):
    return pl.pallas_call(
        kernel,
        out_shape=out,
        in_specs=[pl.BlockSpec(memory_space=space)] * len(args),
        scratch_shapes=scratch,
        out_specs=jax.tree.map(lambda _: pl.BlockSpec(memory_space=pltpu.VMEM), out),
        compiler_params=pltpu.CompilerParams(vmem_limit_bytes=GRANT),
        name=kernel.func.__name__ if isinstance(kernel, functools.partial) else kernel.__name__,
    )(*args)


def shape(*dims, dtype=f32):
    return jax.ShapeDtypeStruct(dims, dtype)


def pack_rows(cap, ids_in, lab_in, emb_in, out_ref, ids_ref, lab_ref, emb_ref, sems):
    copies = [
        pltpu.make_async_copy(src, dst, sems.at[k])
        for k, (src, dst) in enumerate(
            ((ids_in, ids_ref), (lab_in, lab_ref), (emb_in, emb_ref))
        )
    ]
    for copy in copies:
        copy.start()
    rows = emb_ref.shape[0]
    heads = lax.broadcasted_iota(jnp.int32, (PEERS, rows), 0)
    earlier = lax.broadcasted_iota(jnp.int32, (rows, rows), 0) < lax.broadcasted_iota(
        jnp.int32, (rows, rows), 1
    )
    earlier = earlier.astype(f32).astype(bf16)
    copies[0].wait()
    copies[1].wait()
    ids = ids_ref[...]
    mem_f = (heads == ids).astype(f32)
    before = nn(mem_f.astype(bf16), earlier)
    rank = jnp.sum(before * mem_f, axis=0, keepdims=True).astype(jnp.int32)
    at_rank = lax.broadcasted_iota(jnp.int32, (cap, rows), 0) == rank
    tags = (lab_ref[...] + 1).astype(f32)
    tag_slots = nt((mem_f * tags).astype(bf16), at_rank.astype(f32).astype(bf16))
    copies[2].wait()
    emb = emb_ref[...]
    across = emb.shape[1] // LANES
    for p in range(PEERS):
        pick = (at_rank & (ids == p)).astype(f32).astype(bf16)
        picked = nn(pick, emb).astype(bf16)
        for down in range(cap // DEEP):
            for over in range(across):
                out_ref[p, down * across + over] = picked[
                    down * DEEP : (down + 1) * DEEP, over * LANES : (over + 1) * LANES
                ]
        out_ref[p, cap // DEEP * across] = jnp.broadcast_to(
            tag_slots[p : p + 1], (DEEP, cap)
        ).astype(bf16)


def take_rows(cap, got_ref, w_ref, rows_ref, tags_ref, out_ref):
    across = rows_ref.shape[1] // LANES
    for p in range(PEERS):
        for down in range(cap // DEEP):
            for over in range(across):
                at = p * cap + down * DEEP
                rows_ref[at : at + DEEP, over * LANES : (over + 1) * LANES] = got_ref[
                    p, down * across + over
                ]
        tags_ref[:, p * cap : (p + 1) * cap] = got_ref[p, cap // DEEP * across].astype(f32)[:1]
    send(out_ref, nt(rep(w_ref[...]).astype(bf16), rows_ref[...])[:1])


def to_residual(got_ref, tags_ref, rows_ref, curv_ref, out_ref):
    logits = total_of(got_ref)
    tags = tags_ref[...]
    valid = tags > 0.0
    prob = jax.nn.sigmoid(logits)
    residual = jnp.where(valid, prob - jnp.maximum(tags - 1.0, 0.0), 0.0)
    curv_ref[...] = jnp.where(valid, prob * (1.0 - prob), 0.0)
    part = nn(rep(residual).astype(bf16), rows_ref[...])[:1]
    send(out_ref, part, lanes(row_sum(valid.astype(f32))))


def own_share(row, share):
    width = row.shape[1]
    at = lax.axis_index("samp") * share
    return pltpu.roll(row, lax.rem(width - at, width), 1)[:, :share]


def to_direction(got_ref, w_ref, rows_ref, grad_ref, count_ref, share_ref, out_ref):
    width = rows_ref.shape[1]
    total = total_of(got_ref)
    count = total[:, width : width + 1]
    grad = total[:, :width] / count + penalty * w_ref[...]
    grad_ref[...] = grad
    count_ref[...] = lanes(count)
    share_ref[...] = own_share(grad, share_ref.shape[1])
    part = nt(rep(-grad).astype(bf16), rows_ref[...])[:1]
    send(out_ref, part, lanes(row_sum(grad * grad)))


def to_image(got_ref, curv_ref, rows_ref, sq_norm_ref, out_ref):
    slots = rows_ref.shape[0]
    total = total_of(got_ref)
    sq_norm_ref[...] = total[:, slots:]
    proj = total[:, :slots]
    curv = curv_ref[...]
    weighted = (curv * proj).astype(bf16).astype(f32)
    part = nn(rep(weighted).astype(bf16), rows_ref[...])[:1]
    send(out_ref, part, lanes(row_sum(weighted * proj)), jnp.sqrt(curv) * proj)


def to_second(got_ref, sq_norm_ref, curv_ref, grad_ref, count_ref, rows_ref, keep_ref, out_ref):
    width, cap = rows_ref.shape[1], rows_ref.shape[0] // PEERS
    total = got_ref[0, :, : width + LANES]
    for p in range(1, PEERS):
        total = total + got_ref[p, :, : width + LANES]
    count = count_ref[:, :1]
    sq_norm = sq_norm_ref[:, :1]
    direction = -grad_ref[...]
    image = total[:, :width] / count + penalty * direction
    step = sq_norm / (total[:, width : width + 1] / count + penalty * sq_norm)
    resid = direction - step * image
    keep_ref[:, :LANES] = lanes(step)
    keep_ref[:, LANES:] = own_share(resid, keep_ref.shape[1] - LANES)
    part = nt(rep(resid).astype(bf16), rows_ref[...]) * jnp.sqrt(curv_ref[...])
    source = lax.broadcasted_iota(jnp.int32, (PEERS, cap), 0)
    tile = part[:, :cap]
    for p in range(1, PEERS):
        tile = jnp.where(source == p, part[:, p * cap : (p + 1) * cap], tile)
    tile = tile.astype(bf16)
    for peer in range(out_ref.shape[0]):
        out_ref[peer] = tile


def to_step(got_ref, first_ref, count_ref, sq_norm_ref, keep_ref, share_ref, out_ref, grad_ref, tiles_ref):
    groups, _, cap = tiles_ref.shape
    feats = got_ref.shape[0] // groups
    start = first_ref.shape[2] - PEERS * cap
    for s in range(groups):
        for p in range(PEERS):
            tiles_ref[s, p : p + 1, :] = first_ref[s, :, start + p * cap : start + (p + 1) * cap]
    first_sq, cross, second_sq = 0.0, 0.0, 0.0
    for s in range(groups):
        first = tiles_ref[s]
        second = got_ref[s].astype(f32)
        for f in range(1, feats):
            second = second + got_ref[f * groups + s].astype(f32)
        first_sq = first_sq + first * first
        cross = cross + first * second
        second_sq = second_sq + second * second
    first_sq, cross, second_sq = (
        jnp.sum(row_sum(v), axis=0, keepdims=True) for v in (first_sq, cross, second_sq)
    )
    count, sq_norm, first_step = count_ref[:, :1], sq_norm_ref[:, :1], keep_ref[:, :1]
    sq_next = jnp.maximum(-first_step * cross / count, 0.0)
    beta = sq_next / sq_norm
    bend = jnp.maximum(second_sq + 2.0 * beta * cross + beta * beta * first_sq, 0.0)
    below = bend / count + penalty * (sq_next + beta * beta * sq_norm)
    step = jnp.where(sq_next > 0.0, sq_next / jnp.where(sq_next > 0.0, below, 1.0), 0.0)
    grad_ref[...] = share_ref[...]
    direction = -share_ref[...]
    out_ref[...] = first_step * direction + step * (keep_ref[:, LANES:] + beta * direction)


def exchange(values, axis):
    return lax.all_to_all(values, axis, split_axis=0, concat_axis=0, tiled=True)


def shards(embeddings, plant_ids, labels, weights):
    rows_here, width = embeddings.shape
    samps = lax.axis_size("samp")
    share = width // samps
    cap = 2 * rows_here // PEERS
    slots = PEERS * cap

    sent = call(
        functools.partial(pack_rows, cap),
        *(
            pltpu.with_memory_space_constraint(v, pltpu.HBM)
            for v in (plant_ids.reshape(1, rows_here), labels.reshape(1, rows_here), embeddings)
        ),
        out=shape(PEERS, cap // DEEP * (width // LANES) + 1, DEEP, LANES, dtype=bf16),
        scratch=(
            pltpu.VMEM((1, rows_here), jnp.int32),
            pltpu.VMEM((1, rows_here), jnp.int32),
            pltpu.VMEM((rows_here, width), bf16),
            pltpu.SemaphoreType.DMA((3,)),
        ),
        space=pltpu.HBM,
    )
    got = exchange(sent, "plant")
    rows, tags, part = call(
        functools.partial(take_rows, cap),
        got,
        weights,
        out=(shape(slots, width, dtype=bf16), shape(1, slots), shape(PEERS, 1, slots)),
    )
    got = exchange(part, "feat")
    curv, part = call(
        to_residual, got, tags, rows, out=(shape(1, slots), shape(PEERS, 1, width + LANES))
    )
    got = exchange(part, "samp")
    grad, count, grad_share, part = call(
        to_direction,
        got,
        weights,
        rows,
        out=(
            shape(1, width),
            shape(1, LANES),
            shape(1, share),
            shape(PEERS, 1, slots + LANES),
        ),
    )
    got = exchange(part, "feat")
    sq_norm, first = call(
        to_image,
        got,
        curv,
        rows,
        out=(shape(1, LANES), shape(PEERS, 1, width + LANES + slots)),
    )
    first = exchange(first, "samp")
    keep, part = call(
        to_second,
        first,
        sq_norm,
        curv,
        grad,
        count,
        rows,
        out=(
            shape(1, LANES + share),
            shape(lax.axis_size("feat") * samps, PEERS, cap, dtype=bf16),
        ),
    )
    got = exchange(part, ("feat", "samp"))
    return call(
        to_step,
        got,
        first,
        count,
        sq_norm,
        keep,
        grad_share,
        out=(shape(1, share), shape(1, share)),
        scratch=(pltpu.VMEM((samps, PEERS, cap), f32),),
    )


def solution(mesh):
    placed = (
        P(("plant", "samp"), "feat"),
        P(("plant", "samp"), None),
        P(("plant", "samp")),
        P("plant", "feat"),
    )
    return jax.shard_map(
        shards,
        mesh=mesh,
        in_specs=placed,
        out_specs=(P("plant", ("feat", "samp")), P("plant", ("feat", "samp"))),
        check_vma=False,
    )
```

```python
import functools

import jax
import jax.numpy as jnp
from jax import lax
from jax.experimental import pallas as pl
from jax.experimental.pallas import tpu as pltpu
from jax.sharding import PartitionSpec as P

penalty = 0.1
PEERS = 8
LANES = 128
DEEP = 16
GRANT = 12 << 20
f32 = jnp.float32
bf16 = jnp.bfloat16


def nt(a, b):
    return lax.dot_general(a, b, (((1,), (1,)), ((), ())), preferred_element_type=f32)


def nn(a, b):
    return lax.dot_general(a, b, (((1,), (0,)), ((), ())), preferred_element_type=f32)


def rep(row):
    return jnp.broadcast_to(row, (PEERS, row.shape[1]))


def total_of(ref):
    parts = [ref[p] for p in range(PEERS)]
    while len(parts) > 1:
        parts = [a + b for a, b in zip(parts[::2], parts[1::2])]
    return parts[0]


def send(ref, *rows):
    at = 0
    for row in rows:
        for p in range(PEERS):
            ref[p, :, at : at + row.shape[1]] = row
        at = at + row.shape[1]


def lanes(scalar):
    return jnp.broadcast_to(scalar, (1, LANES))


def row_sum(row):
    return jnp.sum(row, axis=1, keepdims=True)


def call(kernel, *args, out, scratch=(), space=pltpu.VMEM):
    return pl.pallas_call(
        kernel,
        out_shape=out,
        in_specs=[pl.BlockSpec(memory_space=space)] * len(args),
        scratch_shapes=scratch,
        out_specs=jax.tree.map(lambda _: pl.BlockSpec(memory_space=pltpu.VMEM), out),
        compiler_params=pltpu.CompilerParams(vmem_limit_bytes=GRANT),
        name=kernel.func.__name__ if isinstance(kernel, functools.partial) else kernel.__name__,
    )(*args)


def shape(*dims, dtype=f32):
    return jax.ShapeDtypeStruct(dims, dtype)


def pack_rows(cap, ids_in, lab_in, emb_in, out_ref, ids_ref, lab_ref, emb_ref, sems):
    copies = [
        pltpu.make_async_copy(src, dst, sems.at[k])
        for k, (src, dst) in enumerate(
            ((ids_in, ids_ref), (lab_in, lab_ref), (emb_in, emb_ref))
        )
    ]
    for copy in copies:
        copy.start()
    rows = emb_ref.shape[0]
    heads = lax.broadcasted_iota(jnp.int32, (PEERS, rows), 0)
    earlier = lax.broadcasted_iota(jnp.int32, (rows, rows), 0) < lax.broadcasted_iota(
        jnp.int32, (rows, rows), 1
    )
    earlier = earlier.astype(f32).astype(bf16)
    copies[0].wait()
    copies[1].wait()
    ids = ids_ref[...]
    mem_f = (heads == ids).astype(f32)
    before = nn(mem_f.astype(bf16), earlier)
    rank = jnp.sum(before * mem_f, axis=0, keepdims=True).astype(jnp.int32)
    at_rank = lax.broadcasted_iota(jnp.int32, (cap, rows), 0) == rank
    tags = (lab_ref[...] + 1).astype(f32)
    tag_slots = nt((mem_f * tags).astype(bf16), at_rank.astype(f32).astype(bf16))
    copies[2].wait()
    emb = emb_ref[...]
    across = emb.shape[1] // LANES
    for p in range(PEERS):
        pick = (at_rank & (ids == p)).astype(f32).astype(bf16)
        picked = nn(pick, emb).astype(bf16)
        for down in range(cap // DEEP):
            for over in range(across):
                out_ref[p, down * across + over] = picked[
                    down * DEEP : (down + 1) * DEEP, over * LANES : (over + 1) * LANES
                ]
        out_ref[p, cap // DEEP * across] = jnp.broadcast_to(
            tag_slots[p : p + 1], (DEEP, cap)
        ).astype(bf16)


def take_rows(cap, got_ref, w_ref, rows_ref, tags_ref, out_ref):
    across = rows_ref.shape[1] // LANES
    for p in range(PEERS):
        for down in range(cap // DEEP):
            for over in range(across):
                at = p * cap + down * DEEP
                rows_ref[at : at + DEEP, over * LANES : (over + 1) * LANES] = got_ref[
                    p, down * across + over
                ]
        tags_ref[:, p * cap : (p + 1) * cap] = got_ref[p, cap // DEEP * across].astype(f32)[:1]
    send(out_ref, nt(rep(w_ref[...]).astype(bf16), rows_ref[...])[:1])


def to_residual(got_ref, tags_ref, rows_ref, curv_ref, out_ref):
    logits = total_of(got_ref)
    tags = tags_ref[...]
    valid = tags > 0.0
    prob = jax.nn.sigmoid(logits)
    residual = jnp.where(valid, prob - jnp.maximum(tags - 1.0, 0.0), 0.0)
    curv_ref[...] = jnp.where(valid, prob * (1.0 - prob), 0.0)
    part = nn(rep(residual).astype(bf16), rows_ref[...])[:1]
    send(out_ref, part, lanes(row_sum(valid.astype(f32))))


def own_share(row, share):
    width = row.shape[1]
    at = lax.axis_index("samp") * share
    return pltpu.roll(row, lax.rem(width - at, width), 1)[:, :share]


def to_direction(got_ref, w_ref, rows_ref, grad_ref, count_ref, share_ref, out_ref):
    width = rows_ref.shape[1]
    total = total_of(got_ref)
    count = total[:, width : width + 1]
    grad = total[:, :width] / count + penalty * w_ref[...]
    grad_ref[...] = grad
    count_ref[...] = lanes(count)
    share_ref[...] = own_share(grad, share_ref.shape[1])
    part = nt(rep(-grad).astype(bf16), rows_ref[...])[:1]
    send(out_ref, part, lanes(row_sum(grad * grad)))


def to_image(got_ref, curv_ref, rows_ref, proj_ref, out_ref):
    slots = rows_ref.shape[0]
    total = total_of(got_ref)
    proj_ref[...] = total
    proj = total[:, :slots]
    weighted = (curv_ref[...] * proj).astype(bf16).astype(f32)
    part = nn(rep(weighted).astype(bf16), rows_ref[...])[:1]
    send(out_ref, part, lanes(row_sum(weighted * proj)))


def to_second(got_ref, proj_ref, curv_ref, grad_ref, count_ref, rows_ref, keep_ref, out_ref, pair_ref):
    width, slots = rows_ref.shape[1], rows_ref.shape[0]
    half = slots // 2
    total = total_of(got_ref)
    count = count_ref[:, :1]
    sq_norm = proj_ref[:, slots : slots + 1]
    direction = -grad_ref[...]
    image = total[:, :width] / count + penalty * direction
    bend = total[:, width : width + 1]
    step = sq_norm / (bend / count + penalty * sq_norm)
    resid = direction - step * image
    keep_ref[:, :LANES] = lanes(step)
    keep_ref[:, LANES : 2 * LANES] = lanes(bend)
    keep_ref[:, 2 * LANES : 3 * LANES] = lanes(sq_norm)
    keep_ref[:, 3 * LANES :] = own_share(resid, keep_ref.shape[1] - 3 * LANES)
    curv = curv_ref[...]
    part = nt(rep(resid).astype(bf16), rows_ref[...])[:1]
    cross = row_sum(curv * proj_ref[:, :slots] * part)
    scaled = part * jnp.sqrt(curv)
    first = cross.astype(bf16).astype(f32)
    second = (cross - first).astype(bf16).astype(f32)
    third = cross - first - second
    lane = lax.broadcasted_iota(jnp.int32, (1, LANES), 1)
    extra = jnp.where(lane == 0, first, jnp.where(lane == 1, second, jnp.where(lane == 2, third, 0.0)))
    pair_ref[0:1, :half] = scaled[:, :half]
    pair_ref[1:2, :half] = scaled[:, half:]
    pair_ref[0:1, half:] = extra
    pair_ref[1:2, half:] = jnp.zeros((1, LANES), f32)
    pair = pair_ref[...].astype(bf16)
    for peer in range(out_ref.shape[0]):
        out_ref[peer] = pair


def to_step(groups, got_ref, count_ref, keep_ref, share_ref, out_ref, grad_ref):
    feats = got_ref.shape[0] // groups
    half = got_ref.shape[2] - LANES
    cross, second_sq = 0.0, 0.0
    for s in range(groups):
        parts = [got_ref[f * groups + s].astype(f32) for f in range(feats)]
        while len(parts) > 1:
            parts = [a + b for a, b in zip(parts[::2], parts[1::2])]
        cross = cross + parts[0][:, half:]
        second_sq = second_sq + parts[0][:, :half] * parts[0][:, :half]
    cross, second_sq = (jnp.sum(row_sum(v), axis=0, keepdims=True) for v in (cross, second_sq))
    count, sq_norm = count_ref[:, :1], keep_ref[:, 2 * LANES : 2 * LANES + 1]
    first_step, first_sq = keep_ref[:, :1], keep_ref[:, LANES : LANES + 1]
    sq_next = jnp.maximum(-first_step * cross / count, 0.0)
    beta = sq_next / sq_norm
    bend = jnp.maximum(second_sq + 2.0 * beta * cross + beta * beta * first_sq, 0.0)
    below = bend / count + penalty * (sq_next + beta * beta * sq_norm)
    step = jnp.where(sq_next > 0.0, sq_next / jnp.where(sq_next > 0.0, below, 1.0), 0.0)
    grad_ref[...] = share_ref[...]
    direction = -share_ref[...]
    out_ref[...] = first_step * direction + step * (keep_ref[:, 3 * LANES :] + beta * direction)


def exchange(values, axis):
    return lax.all_to_all(values, axis, split_axis=0, concat_axis=0, tiled=True)


def shards(embeddings, plant_ids, labels, weights):
    rows_here, width = embeddings.shape
    samps = lax.axis_size("samp")
    share = width // samps
    cap = 2 * rows_here // PEERS
    slots = PEERS * cap

    sent = call(
        functools.partial(pack_rows, cap),
        *(
            pltpu.with_memory_space_constraint(v, pltpu.HBM)
            for v in (plant_ids.reshape(1, rows_here), labels.reshape(1, rows_here), embeddings)
        ),
        out=shape(PEERS, cap // DEEP * (width // LANES) + 1, DEEP, LANES, dtype=bf16),
        scratch=(
            pltpu.VMEM((1, rows_here), jnp.int32),
            pltpu.VMEM((1, rows_here), jnp.int32),
            pltpu.VMEM((rows_here, width), bf16),
            pltpu.SemaphoreType.DMA((3,)),
        ),
        space=pltpu.HBM,
    )
    got = exchange(sent, "plant")
    rows, tags, part = call(
        functools.partial(take_rows, cap),
        got,
        weights,
        out=(shape(slots, width, dtype=bf16), shape(1, slots), shape(PEERS, 1, slots)),
    )
    got = exchange(part, "feat")
    curv, part = call(
        to_residual, got, tags, rows, out=(shape(1, slots), shape(PEERS, 1, width + LANES))
    )
    got = exchange(part, "samp")
    grad, count, grad_share, part = call(
        to_direction,
        got,
        weights,
        rows,
        out=(
            shape(1, width),
            shape(1, LANES),
            shape(1, share),
            shape(PEERS, 1, slots + LANES),
        ),
    )
    got = exchange(part, "feat")
    proj, part = call(
        to_image, got, curv, rows, out=(shape(1, slots + LANES), shape(PEERS, 1, width + LANES))
    )
    got = exchange(part, "samp")
    pair = (2, slots // 2 + LANES)
    keep, part = call(
        to_second,
        got,
        proj,
        curv,
        grad,
        count,
        rows,
        out=(
            shape(1, 3 * LANES + share),
            shape(lax.axis_size("feat") * samps, *pair, dtype=bf16),
        ),
        scratch=(pltpu.VMEM(pair, f32),),
    )
    got = exchange(part, ("feat", "samp"))
    return call(
        functools.partial(to_step, samps),
        got,
        count,
        keep,
        grad_share,
        out=(shape(1, share), shape(1, share)),
    )


def solution(mesh):
    placed = (
        P(("plant", "samp"), "feat"),
        P(("plant", "samp"), None),
        P(("plant", "samp")),
        P("plant", "feat"),
    )
    return jax.shard_map(
        shards,
        mesh=mesh,
        in_specs=placed,
        out_specs=(P("plant", ("feat", "samp")), P("plant", ("feat", "samp"))),
        check_vma=False,
    )
```

```python
import functools

import jax
import jax.numpy as jnp
from jax import lax
from jax.experimental import pallas as pl
from jax.experimental.pallas import tpu as pltpu
from jax.sharding import PartitionSpec as P

penalty = 0.1
PEERS = 8
LANES = 128
DEEP = 16
GRANT = 12 << 20
f32 = jnp.float32
bf16 = jnp.bfloat16


def nt(a, b):
    return lax.dot_general(a, b, (((1,), (1,)), ((), ())), preferred_element_type=f32)


def nn(a, b):
    return lax.dot_general(a, b, (((1,), (0,)), ((), ())), preferred_element_type=f32)


def rep(row):
    return jnp.broadcast_to(row, (PEERS, row.shape[1]))


def total_of(ref):
    parts = [ref[p] for p in range(PEERS)]
    while len(parts) > 1:
        parts = [a + b for a, b in zip(parts[::2], parts[1::2])]
    return parts[0]


def send(ref, *rows):
    at = 0
    for row in rows:
        for p in range(PEERS):
            ref[p, :, at : at + row.shape[1]] = row
        at = at + row.shape[1]


def lanes(scalar):
    return jnp.broadcast_to(scalar, (1, LANES))


def row_sum(row):
    return jnp.sum(row, axis=1, keepdims=True)


def call(kernel, *args, out, scratch=(), space=pltpu.VMEM):
    return pl.pallas_call(
        kernel,
        out_shape=out,
        in_specs=[pl.BlockSpec(memory_space=space)] * len(args),
        scratch_shapes=scratch,
        out_specs=jax.tree.map(lambda _: pl.BlockSpec(memory_space=pltpu.VMEM), out),
        compiler_params=pltpu.CompilerParams(vmem_limit_bytes=GRANT),
        name=kernel.func.__name__ if isinstance(kernel, functools.partial) else kernel.__name__,
    )(*args)


def shape(*dims, dtype=f32):
    return jax.ShapeDtypeStruct(dims, dtype)


def pack_rows(cap, ids_in, lab_in, emb_in, out_ref, ids_ref, lab_ref, emb_ref, sems):
    copies = [
        pltpu.make_async_copy(src, dst, sems.at[k])
        for k, (src, dst) in enumerate(
            ((ids_in, ids_ref), (lab_in, lab_ref), (emb_in, emb_ref))
        )
    ]
    for copy in copies:
        copy.start()
    rows = emb_ref.shape[0]
    heads = lax.broadcasted_iota(jnp.int32, (PEERS, rows), 0)
    earlier = lax.broadcasted_iota(jnp.int32, (rows, rows), 0) < lax.broadcasted_iota(
        jnp.int32, (rows, rows), 1
    )
    earlier = earlier.astype(f32).astype(bf16)
    copies[0].wait()
    copies[1].wait()
    ids = ids_ref[...]
    mem_f = (heads == ids).astype(f32)
    before = nn(mem_f.astype(bf16), earlier)
    rank = jnp.sum(before * mem_f, axis=0, keepdims=True).astype(jnp.int32)
    at_rank = lax.broadcasted_iota(jnp.int32, (cap, rows), 0) == rank
    tags = (lab_ref[...] + 1).astype(f32)
    tag_slots = nt((mem_f * tags).astype(bf16), at_rank.astype(f32).astype(bf16))
    copies[2].wait()
    emb = emb_ref[...]
    across = emb.shape[1] // LANES
    for p in range(PEERS):
        pick = (at_rank & (ids == p)).astype(f32).astype(bf16)
        picked = nn(pick, emb).astype(bf16)
        for down in range(cap // DEEP):
            for over in range(across):
                out_ref[p, down * across + over] = picked[
                    down * DEEP : (down + 1) * DEEP, over * LANES : (over + 1) * LANES
                ]
        out_ref[p, cap // DEEP * across] = jnp.broadcast_to(
            tag_slots[p : p + 1], (DEEP, cap)
        ).astype(bf16)


def take_rows(cap, got_ref, w_ref, rows_ref, tags_ref, out_ref):
    across = rows_ref.shape[1] // LANES
    for p in range(PEERS):
        for down in range(cap // DEEP):
            for over in range(across):
                at = p * cap + down * DEEP
                rows_ref[at : at + DEEP, over * LANES : (over + 1) * LANES] = got_ref[
                    p, down * across + over
                ]
        tags_ref[:, p * cap : (p + 1) * cap] = got_ref[p, cap // DEEP * across].astype(f32)[:1]
    send(out_ref, nt(rep(w_ref[...]).astype(bf16), rows_ref[...])[:1])


def to_residual(got_ref, tags_ref, rows_ref, curv_ref, out_ref):
    logits = total_of(got_ref)
    tags = tags_ref[...]
    valid = tags > 0.0
    prob = jax.nn.sigmoid(logits)
    residual = jnp.where(valid, prob - jnp.maximum(tags - 1.0, 0.0), 0.0)
    curv_ref[...] = jnp.where(valid, prob * (1.0 - prob), 0.0)
    part = nn(rep(residual).astype(bf16), rows_ref[...])[:1]
    send(out_ref, part, lanes(row_sum(valid.astype(f32))))


def own_share(row, share):
    width = row.shape[1]
    at = lax.axis_index("samp") * share
    return pltpu.roll(row, lax.rem(width - at, width), 1)[:, :share]


def to_direction(got_ref, w_ref, rows_ref, grad_ref, count_ref, share_ref, out_ref):
    width = rows_ref.shape[1]
    total = total_of(got_ref)
    count = total[:, width : width + 1]
    grad = total[:, :width] / count + penalty * w_ref[...]
    grad_ref[...] = grad
    count_ref[...] = lanes(count)
    share_ref[...] = own_share(grad, share_ref.shape[1])
    part = nt(rep(-grad).astype(bf16), rows_ref[...])[:1]
    send(out_ref, part, lanes(row_sum(grad * grad)))


def to_image(got_ref, curv_ref, rows_ref, proj_ref, out_ref):
    slots = rows_ref.shape[0]
    total = total_of(got_ref)
    proj_ref[...] = total
    proj = total[:, :slots]
    weighted = (curv_ref[...] * proj).astype(bf16).astype(f32)
    part = nn(rep(weighted).astype(bf16), rows_ref[...])[:1]
    send(out_ref, part, lanes(row_sum(weighted * proj)))


def to_second(got_ref, proj_ref, curv_ref, grad_ref, count_ref, rows_ref, keep_ref, out_ref, pair_ref):
    width, slots = rows_ref.shape[1], rows_ref.shape[0]
    half = slots // 2
    total = total_of(got_ref)
    count = count_ref[:, :1]
    sq_norm = proj_ref[:, slots : slots + 1]
    direction = -grad_ref[...]
    image = total[:, :width] / count + penalty * direction
    bend = total[:, width : width + 1]
    step = sq_norm / (bend / count + penalty * sq_norm)
    resid = direction - step * image
    keep_ref[:, :LANES] = lanes(step)
    keep_ref[:, LANES : 2 * LANES] = lanes(bend)
    keep_ref[:, 2 * LANES : 3 * LANES] = lanes(sq_norm)
    keep_ref[:, 3 * LANES :] = own_share(resid, keep_ref.shape[1] - 3 * LANES)
    curv = curv_ref[...]
    part = nt(rep(resid).astype(bf16), rows_ref[...])[:1]
    cross = row_sum(curv * proj_ref[:, :slots] * part)
    scaled = part * jnp.sqrt(curv)
    first = cross.astype(bf16).astype(f32)
    second = (cross - first).astype(bf16).astype(f32)
    third = cross - first - second
    lane = lax.broadcasted_iota(jnp.int32, (1, LANES), 1)
    extra = jnp.where(lane == 0, first, jnp.where(lane == 1, second, jnp.where(lane == 2, third, 0.0)))
    pair_ref[0:1, :half] = scaled[:, :half]
    pair_ref[1:2, :half] = scaled[:, half:]
    pair_ref[0:1, half:] = extra
    pair_ref[1:2, half:] = jnp.zeros((1, LANES), f32)
    pair = pair_ref[...].astype(bf16)
    for peer in range(out_ref.shape[0]):
        out_ref[peer] = pair


def to_step(groups, got_ref, count_ref, keep_ref, share_ref, out_ref, grad_ref):
    feats = got_ref.shape[0] // groups
    half = got_ref.shape[2] - LANES
    cross, second_sq = 0.0, 0.0
    for s in range(groups):
        parts = [got_ref[s * feats + f].astype(f32) for f in range(feats)]
        while len(parts) > 1:
            parts = [a + b for a, b in zip(parts[::2], parts[1::2])]
        cross = cross + parts[0][:, half:]
        second_sq = second_sq + parts[0][:, :half] * parts[0][:, :half]
    cross, second_sq = (jnp.sum(row_sum(v), axis=0, keepdims=True) for v in (cross, second_sq))
    count, sq_norm = count_ref[:, :1], keep_ref[:, 2 * LANES : 2 * LANES + 1]
    first_step, first_sq = keep_ref[:, :1], keep_ref[:, LANES : LANES + 1]
    sq_next = jnp.maximum(-first_step * cross / count, 0.0)
    beta = sq_next / sq_norm
    bend = jnp.maximum(second_sq + 2.0 * beta * cross + beta * beta * first_sq, 0.0)
    below = bend / count + penalty * (sq_next + beta * beta * sq_norm)
    step = jnp.where(sq_next > 0.0, sq_next / jnp.where(sq_next > 0.0, below, 1.0), 0.0)
    grad_ref[...] = share_ref[...]
    direction = -share_ref[...]
    out_ref[...] = first_step * direction + step * (keep_ref[:, 3 * LANES :] + beta * direction)


def exchange(values, axis):
    return lax.all_to_all(values, axis, split_axis=0, concat_axis=0, tiled=True)


def shards(embeddings, plant_ids, labels, weights):
    rows_here, width = embeddings.shape
    samps = lax.axis_size("samp")
    share = width // samps
    cap = 2 * rows_here // PEERS
    slots = PEERS * cap

    sent = call(
        functools.partial(pack_rows, cap),
        *(
            pltpu.with_memory_space_constraint(v, pltpu.HBM)
            for v in (plant_ids.reshape(1, rows_here), labels.reshape(1, rows_here), embeddings)
        ),
        out=shape(PEERS, cap // DEEP * (width // LANES) + 1, DEEP, LANES, dtype=bf16),
        scratch=(
            pltpu.VMEM((1, rows_here), jnp.int32),
            pltpu.VMEM((1, rows_here), jnp.int32),
            pltpu.VMEM((rows_here, width), bf16),
            pltpu.SemaphoreType.DMA((3,)),
        ),
        space=pltpu.HBM,
    )
    got = exchange(sent, "plant")
    rows, tags, part = call(
        functools.partial(take_rows, cap),
        got,
        weights,
        out=(shape(slots, width, dtype=bf16), shape(1, slots), shape(PEERS, 1, slots)),
    )
    got = exchange(part, "feat")
    curv, part = call(
        to_residual, got, tags, rows, out=(shape(1, slots), shape(PEERS, 1, width + LANES))
    )
    got = exchange(part, "samp")
    grad, count, grad_share, part = call(
        to_direction,
        got,
        weights,
        rows,
        out=(
            shape(1, width),
            shape(1, LANES),
            shape(1, share),
            shape(PEERS, 1, slots + LANES),
        ),
    )
    got = exchange(part, "feat")
    proj, part = call(
        to_image, got, curv, rows, out=(shape(1, slots + LANES), shape(PEERS, 1, width + LANES))
    )
    got = exchange(part, "samp")
    pair = (2, slots // 2 + LANES)
    keep, part = call(
        to_second,
        got,
        proj,
        curv,
        grad,
        count,
        rows,
        out=(
            shape(1, 3 * LANES + share),
            shape(lax.axis_size("feat") * samps, *pair, dtype=bf16),
        ),
        scratch=(pltpu.VMEM(pair, f32),),
    )
    got = exchange(part, ("samp", "feat"))
    return call(
        functools.partial(to_step, samps),
        got,
        count,
        keep,
        grad_share,
        out=(shape(1, share), shape(1, share)),
    )


def solution(mesh):
    placed = (
        P(("plant", "samp"), "feat"),
        P(("plant", "samp"), None),
        P(("plant", "samp")),
        P("plant", "feat"),
    )
    return jax.shard_map(
        shards,
        mesh=mesh,
        in_specs=placed,
        out_specs=(P("plant", ("feat", "samp")), P("plant", ("feat", "samp"))),
        check_vma=False,
    )
```

```python
import functools

import jax
import jax.numpy as jnp
from jax import lax
from jax.experimental import pallas as pl
from jax.experimental.pallas import tpu as pltpu
from jax.sharding import PartitionSpec as P

penalty = 0.1
PEERS = 8
LANES = 128
DEEP = 16
GRANT = 12 << 20
f32 = jnp.float32
bf16 = jnp.bfloat16


def nt(a, b):
    return lax.dot_general(a, b, (((1,), (1,)), ((), ())), preferred_element_type=f32)


def nn(a, b):
    return lax.dot_general(a, b, (((1,), (0,)), ((), ())), preferred_element_type=f32)


def rep(row):
    return jnp.broadcast_to(row, (PEERS, row.shape[1]))


def total_of(ref):
    parts = [ref[p] for p in range(PEERS)]
    while len(parts) > 1:
        parts = [a + b for a, b in zip(parts[::2], parts[1::2])]
    return parts[0]


def send(ref, *rows):
    at = 0
    for row in rows:
        for p in range(PEERS):
            ref[p, :, at : at + row.shape[1]] = row
        at = at + row.shape[1]


def lanes(scalar):
    return jnp.broadcast_to(scalar, (1, LANES))


def row_sum(row):
    return jnp.sum(row, axis=1, keepdims=True)


def call(kernel, *args, out, scratch=(), space=pltpu.VMEM):
    return pl.pallas_call(
        kernel,
        out_shape=out,
        in_specs=[pl.BlockSpec(memory_space=space)] * len(args),
        scratch_shapes=scratch,
        out_specs=jax.tree.map(lambda _: pl.BlockSpec(memory_space=pltpu.VMEM), out),
        compiler_params=pltpu.CompilerParams(vmem_limit_bytes=GRANT),
        name=kernel.func.__name__ if isinstance(kernel, functools.partial) else kernel.__name__,
    )(*args)


def shape(*dims, dtype=f32):
    return jax.ShapeDtypeStruct(dims, dtype)


def pack_rows(cap, ids_in, lab_in, emb_in, out_ref, ids_ref, lab_ref, emb_ref, sems):
    copies = [
        pltpu.make_async_copy(src, dst, sems.at[k])
        for k, (src, dst) in enumerate(
            ((ids_in, ids_ref), (lab_in, lab_ref), (emb_in, emb_ref))
        )
    ]
    for copy in copies:
        copy.start()
    rows = emb_ref.shape[0]
    heads = lax.broadcasted_iota(jnp.int32, (PEERS, rows), 0)
    earlier = lax.broadcasted_iota(jnp.int32, (rows, rows), 0) < lax.broadcasted_iota(
        jnp.int32, (rows, rows), 1
    )
    earlier = earlier.astype(f32).astype(bf16)
    copies[0].wait()
    copies[1].wait()
    ids = ids_ref[...]
    mem_f = (heads == ids).astype(f32)
    before = nn(mem_f.astype(bf16), earlier)
    rank = jnp.sum(before * mem_f, axis=0, keepdims=True).astype(jnp.int32)
    at_rank = lax.broadcasted_iota(jnp.int32, (cap, rows), 0) == rank
    tags = (lab_ref[...] + 1).astype(f32)
    tag_slots = nt((mem_f * tags).astype(bf16), at_rank.astype(f32).astype(bf16))
    copies[2].wait()
    emb = emb_ref[...]
    across = emb.shape[1] // LANES
    for p in range(PEERS):
        pick = (at_rank & (ids == p)).astype(f32).astype(bf16)
        picked = nn(pick, emb).astype(bf16)
        for down in range(cap // DEEP):
            for over in range(across):
                out_ref[p, down * across + over] = picked[
                    down * DEEP : (down + 1) * DEEP, over * LANES : (over + 1) * LANES
                ]
        out_ref[p, cap // DEEP * across] = jnp.broadcast_to(
            tag_slots[p : p + 1], (DEEP, cap)
        ).astype(bf16)


def take_rows(cap, got_ref, w_ref, rows_ref, tags_ref, out_ref):
    across = rows_ref.shape[1] // LANES
    for p in range(PEERS):
        for down in range(cap // DEEP):
            for over in range(across):
                at = p * cap + down * DEEP
                rows_ref[at : at + DEEP, over * LANES : (over + 1) * LANES] = got_ref[
                    p, down * across + over
                ]
        tags_ref[:, p * cap : (p + 1) * cap] = got_ref[p, cap // DEEP * across].astype(f32)[:1]
    send(out_ref, nt(rep(w_ref[...]).astype(bf16), rows_ref[...])[:1])


def to_residual(got_ref, tags_ref, rows_ref, curv_ref, out_ref):
    logits = total_of(got_ref)
    tags = tags_ref[...]
    valid = tags > 0.0
    prob = jax.nn.sigmoid(logits)
    residual = jnp.where(valid, prob - jnp.maximum(tags - 1.0, 0.0), 0.0)
    curv_ref[...] = jnp.where(valid, prob * (1.0 - prob), 0.0)
    part = nn(rep(residual).astype(bf16), rows_ref[...])[:1]
    send(out_ref, part, lanes(row_sum(valid.astype(f32))))


def own_share(row, share):
    width = row.shape[1]
    at = lax.axis_index("samp") * share
    return pltpu.roll(row, lax.rem(width - at, width), 1)[:, :share]


def to_direction(got_ref, w_ref, rows_ref, grad_ref, count_ref, share_ref, out_ref):
    width = rows_ref.shape[1]
    total = total_of(got_ref)
    count = total[:, width : width + 1]
    grad = total[:, :width] / count + penalty * w_ref[...]
    grad_ref[...] = grad
    count_ref[...] = lanes(count)
    share_ref[...] = own_share(grad, share_ref.shape[1])
    part = nt(rep(-grad).astype(bf16), rows_ref[...])[:1]
    send(out_ref, part, lanes(row_sum(grad * grad)))


def to_image(got_ref, curv_ref, rows_ref, proj_ref, out_ref):
    slots = rows_ref.shape[0]
    total = total_of(got_ref)
    proj_ref[...] = total
    proj = total[:, :slots]
    weighted = (curv_ref[...] * proj).astype(bf16).astype(f32)
    part = nn(rep(weighted).astype(bf16), rows_ref[...])[:1]
    send(out_ref, part, lanes(row_sum(weighted * proj)))


def to_second(got_ref, proj_ref, curv_ref, grad_ref, count_ref, rows_ref, keep_ref, out_ref, pair_ref):
    width, slots = rows_ref.shape[1], rows_ref.shape[0]
    half = slots // 2
    total = total_of(got_ref)
    count = count_ref[:, :1]
    sq_norm = proj_ref[:, slots : slots + 1]
    direction = -grad_ref[...]
    image = total[:, :width] / count + penalty * direction
    bend = total[:, width : width + 1]
    step = sq_norm / (bend / count + penalty * sq_norm)
    resid = direction - step * image
    keep_ref[:, :LANES] = lanes(step)
    keep_ref[:, LANES : 2 * LANES] = lanes(bend)
    keep_ref[:, 2 * LANES : 3 * LANES] = lanes(sq_norm)
    keep_ref[:, 3 * LANES :] = own_share(resid, keep_ref.shape[1] - 3 * LANES)
    curv = curv_ref[...]
    part = nt(rep(resid).astype(bf16), rows_ref[...])[:1]
    cross = row_sum(curv * proj_ref[:, :slots] * part)
    scaled = part * jnp.sqrt(curv)
    first = cross.astype(bf16).astype(f32)
    second = (cross - first).astype(bf16).astype(f32)
    third = cross - first - second
    lane = lax.broadcasted_iota(jnp.int32, (1, LANES), 1)
    extra = jnp.where(lane == 0, first, jnp.where(lane == 1, second, jnp.where(lane == 2, third, 0.0)))
    pair_ref[0:1, :half] = scaled[:, :half]
    pair_ref[1:2, :half] = scaled[:, half:]
    pair_ref[0:1, half:] = extra
    pair_ref[1:2, half:] = jnp.zeros((1, LANES), f32)
    pair = pair_ref[...].astype(bf16)
    for peer in range(out_ref.shape[0]):
        out_ref[peer] = pair


def to_step(groups, got_ref, count_ref, keep_ref, share_ref, out_ref, grad_ref):
    feats = got_ref.shape[0] // groups
    half = got_ref.shape[2] - LANES
    cross, second_sq = 0.0, 0.0
    for s in range(groups):
        parts = [got_ref[(s - f) % groups * feats + f].astype(f32) for f in range(feats)]
        while len(parts) > 1:
            parts = [a + b for a, b in zip(parts[::2], parts[1::2])]
        cross = cross + parts[0][:, half:]
        second_sq = second_sq + parts[0][:, :half] * parts[0][:, :half]
    cross, second_sq = (jnp.sum(row_sum(v), axis=0, keepdims=True) for v in (cross, second_sq))
    count, sq_norm = count_ref[:, :1], keep_ref[:, 2 * LANES : 2 * LANES + 1]
    first_step, first_sq = keep_ref[:, :1], keep_ref[:, LANES : LANES + 1]
    sq_next = jnp.maximum(-first_step * cross / count, 0.0)
    beta = sq_next / sq_norm
    bend = jnp.maximum(second_sq + 2.0 * beta * cross + beta * beta * first_sq, 0.0)
    below = bend / count + penalty * (sq_next + beta * beta * sq_norm)
    step = jnp.where(sq_next > 0.0, sq_next / jnp.where(sq_next > 0.0, below, 1.0), 0.0)
    grad_ref[...] = share_ref[...]
    direction = -share_ref[...]
    out_ref[...] = first_step * direction + step * (keep_ref[:, 3 * LANES :] + beta * direction)


def exchange(values, axis, groups=None):
    return lax.all_to_all(
        values, axis, split_axis=0, concat_axis=0, tiled=True, axis_index_groups=groups
    )


def shards(embeddings, plant_ids, labels, weights):
    rows_here, width = embeddings.shape
    samps = lax.axis_size("samp")
    share = width // samps
    cap = 2 * rows_here // PEERS
    slots = PEERS * cap

    sent = call(
        functools.partial(pack_rows, cap),
        *(
            pltpu.with_memory_space_constraint(v, pltpu.HBM)
            for v in (plant_ids.reshape(1, rows_here), labels.reshape(1, rows_here), embeddings)
        ),
        out=shape(PEERS, cap // DEEP * (width // LANES) + 1, DEEP, LANES, dtype=bf16),
        scratch=(
            pltpu.VMEM((1, rows_here), jnp.int32),
            pltpu.VMEM((1, rows_here), jnp.int32),
            pltpu.VMEM((rows_here, width), bf16),
            pltpu.SemaphoreType.DMA((3,)),
        ),
        space=pltpu.HBM,
    )
    got = exchange(sent, "plant")
    rows, tags, part = call(
        functools.partial(take_rows, cap),
        got,
        weights,
        out=(shape(slots, width, dtype=bf16), shape(1, slots), shape(PEERS, 1, slots)),
    )
    got = exchange(part, "feat")
    curv, part = call(
        to_residual, got, tags, rows, out=(shape(1, slots), shape(PEERS, 1, width + LANES))
    )
    got = exchange(part, "samp")
    grad, count, grad_share, part = call(
        to_direction,
        got,
        weights,
        rows,
        out=(
            shape(1, width),
            shape(1, LANES),
            shape(1, share),
            shape(PEERS, 1, slots + LANES),
        ),
    )
    got = exchange(part, "feat")
    proj, part = call(
        to_image, got, curv, rows, out=(shape(1, slots + LANES), shape(PEERS, 1, width + LANES))
    )
    got = exchange(part, "samp")
    pair = (2, slots // 2 + LANES)
    keep, part = call(
        to_second,
        got,
        proj,
        curv,
        grad,
        count,
        rows,
        out=(
            shape(1, 3 * LANES + share),
            shape(lax.axis_size("feat") * samps, *pair, dtype=bf16),
        ),
        scratch=(pltpu.VMEM(pair, f32),),
    )
    feats = lax.axis_size("feat")
    diagonals = [f * samps + (turn + f) % samps for turn in range(samps) for f in range(feats)]
    got = exchange(part, ("feat", "samp"), [diagonals])
    return call(
        functools.partial(to_step, samps),
        got,
        count,
        keep,
        grad_share,
        out=(shape(1, share), shape(1, share)),
    )


def solution(mesh):
    placed = (
        P(("plant", "samp"), "feat"),
        P(("plant", "samp"), None),
        P(("plant", "samp")),
        P("plant", "feat"),
    )
    return jax.shard_map(
        shards,
        mesh=mesh,
        in_specs=placed,
        out_specs=(P("plant", ("feat", "samp")), P("plant", ("feat", "samp"))),
        check_vma=False,
    )
```

```python
import functools

import jax
import jax.numpy as jnp
from jax import lax
from jax.experimental import pallas as pl
from jax.experimental.pallas import tpu as pltpu
from jax.sharding import PartitionSpec as P

penalty = 0.1
PEERS = 8
LANES = 128
DEEP = 16
GRANT = 12 << 20
f32 = jnp.float32
bf16 = jnp.bfloat16


def nt(a, b):
    return lax.dot_general(a, b, (((1,), (1,)), ((), ())), preferred_element_type=f32)


def nn(a, b):
    return lax.dot_general(a, b, (((1,), (0,)), ((), ())), preferred_element_type=f32)


def rep(row):
    return jnp.broadcast_to(row, (PEERS, row.shape[1]))


def total_of(ref):
    parts = [ref[p] for p in range(PEERS)]
    while len(parts) > 1:
        parts = [a + b for a, b in zip(parts[::2], parts[1::2])]
    return parts[0]


def send(ref, *rows):
    at = 0
    for row in rows:
        for p in range(PEERS):
            ref[p, :, at : at + row.shape[1]] = row
        at = at + row.shape[1]


def lanes(scalar):
    return jnp.broadcast_to(scalar, (1, LANES))


def row_sum(row):
    return jnp.sum(row, axis=1, keepdims=True)


def call(kernel, *args, out, scratch=(), space=pltpu.VMEM):
    return pl.pallas_call(
        kernel,
        out_shape=out,
        in_specs=[pl.BlockSpec(memory_space=space)] * len(args),
        scratch_shapes=scratch,
        out_specs=jax.tree.map(lambda _: pl.BlockSpec(memory_space=pltpu.VMEM), out),
        compiler_params=pltpu.CompilerParams(vmem_limit_bytes=GRANT),
        name=kernel.func.__name__ if isinstance(kernel, functools.partial) else kernel.__name__,
    )(*args)


def shape(*dims, dtype=f32):
    return jax.ShapeDtypeStruct(dims, dtype)


def pack_rows(cap, ids_in, lab_in, emb_in, out_ref, ids_ref, lab_ref, emb_ref, sems):
    copies = [
        pltpu.make_async_copy(src, dst, sems.at[k])
        for k, (src, dst) in enumerate(
            ((ids_in, ids_ref), (lab_in, lab_ref), (emb_in, emb_ref))
        )
    ]
    for copy in copies:
        copy.start()
    rows = emb_ref.shape[0]
    heads = lax.broadcasted_iota(jnp.int32, (PEERS, rows), 0)
    earlier = lax.broadcasted_iota(jnp.int32, (rows, rows), 0) < lax.broadcasted_iota(
        jnp.int32, (rows, rows), 1
    )
    earlier = earlier.astype(f32).astype(bf16)
    copies[0].wait()
    copies[1].wait()
    ids = ids_ref[...]
    mem_f = (heads == ids).astype(f32)
    before = nn(mem_f.astype(bf16), earlier)
    rank = jnp.sum(before * mem_f, axis=0, keepdims=True).astype(jnp.int32)
    at_rank = lax.broadcasted_iota(jnp.int32, (cap, rows), 0) == rank
    tags = (lab_ref[...] + 1).astype(f32)
    tag_slots = nt((mem_f * tags).astype(bf16), at_rank.astype(f32).astype(bf16))
    copies[2].wait()
    emb = emb_ref[...]
    across = emb.shape[1] // LANES
    for p in range(PEERS):
        pick = (at_rank & (ids == p)).astype(f32).astype(bf16)
        picked = nn(pick, emb).astype(bf16)
        for down in range(cap // DEEP):
            for over in range(across):
                out_ref[p, down * across + over] = picked[
                    down * DEEP : (down + 1) * DEEP, over * LANES : (over + 1) * LANES
                ]
        out_ref[p, cap // DEEP * across] = jnp.broadcast_to(
            tag_slots[p : p + 1], (DEEP, cap)
        ).astype(bf16)


def take_rows(cap, got_ref, w_ref, rows_ref, tags_ref, out_ref):
    across = rows_ref.shape[1] // LANES
    for p in range(PEERS):
        for down in range(cap // DEEP):
            for over in range(across):
                at = p * cap + down * DEEP
                rows_ref[at : at + DEEP, over * LANES : (over + 1) * LANES] = got_ref[
                    p, down * across + over
                ]
        tags_ref[:, p * cap : (p + 1) * cap] = got_ref[p, cap // DEEP * across].astype(f32)[:1]
    send(out_ref, nt(rep(w_ref[...]).astype(bf16), rows_ref[...])[:1])


def to_residual(got_ref, tags_ref, rows_ref, curv_ref, out_ref):
    logits = total_of(got_ref)
    tags = tags_ref[...]
    valid = tags > 0.0
    prob = jax.nn.sigmoid(logits)
    residual = jnp.where(valid, prob - jnp.maximum(tags - 1.0, 0.0), 0.0)
    curv_ref[...] = jnp.where(valid, prob * (1.0 - prob), 0.0)
    part = nn(rep(residual).astype(bf16), rows_ref[...])[:1]
    send(out_ref, part, lanes(row_sum(valid.astype(f32))))


def own_share(row, share):
    width = row.shape[1]
    at = lax.axis_index("samp") * share
    return pltpu.roll(row, lax.rem(width - at, width), 1)[:, :share]


def to_direction(got_ref, w_ref, rows_ref, grad_ref, count_ref, share_ref, out_ref):
    width = rows_ref.shape[1]
    total = total_of(got_ref)
    count = total[:, width : width + 1]
    grad = total[:, :width] / count + penalty * w_ref[...]
    grad_ref[...] = grad
    count_ref[...] = lanes(count)
    share_ref[...] = own_share(grad, share_ref.shape[1])
    part = nt(rep(-grad).astype(bf16), rows_ref[...])[:1]
    send(out_ref, part, lanes(row_sum(grad * grad)))


def to_image(got_ref, curv_ref, rows_ref, proj_ref, out_ref):
    slots = rows_ref.shape[0]
    total = total_of(got_ref)
    proj_ref[...] = total
    proj = total[:, :slots]
    weighted = (curv_ref[...] * proj).astype(bf16).astype(f32)
    part = nn(rep(weighted).astype(bf16), rows_ref[...])[:1]
    send(out_ref, part, lanes(row_sum(weighted * proj)))


def to_second(got_ref, proj_ref, curv_ref, grad_ref, count_ref, rows_ref, keep_ref, out_ref, pair_ref):
    width, slots = rows_ref.shape[1], rows_ref.shape[0]
    half = slots // 2
    total = total_of(got_ref)
    count = count_ref[:, :1]
    sq_norm = proj_ref[:, slots : slots + 1]
    direction = -grad_ref[...]
    image = total[:, :width] / count + penalty * direction
    bend = total[:, width : width + 1]
    step = sq_norm / (bend / count + penalty * sq_norm)
    resid = direction - step * image
    keep_ref[:, :LANES] = lanes(step)
    keep_ref[:, LANES : 2 * LANES] = lanes(bend)
    keep_ref[:, 2 * LANES : 3 * LANES] = lanes(sq_norm)
    keep_ref[:, 3 * LANES :] = own_share(resid, keep_ref.shape[1] - 3 * LANES)
    curv = curv_ref[...]
    part = nt(rep(resid).astype(bf16), rows_ref[...])[:1]
    cross = row_sum(curv * proj_ref[:, :slots] * part)
    scaled = part * jnp.sqrt(curv)
    first = cross.astype(bf16).astype(f32)
    second = (cross - first).astype(bf16).astype(f32)
    third = cross - first - second
    lane = lax.broadcasted_iota(jnp.int32, (1, LANES), 1)
    extra = jnp.where(lane == 0, first, jnp.where(lane == 1, second, jnp.where(lane == 2, third, 0.0)))
    pair_ref[0:1, :half] = scaled[:, :half]
    pair_ref[1:2, :half] = scaled[:, half:]
    pair_ref[0:1, half:] = extra
    pair_ref[1:2, half:] = jnp.zeros((1, LANES), f32)
    pair = pair_ref[...].astype(bf16)
    for peer in range(out_ref.shape[0]):
        out_ref[peer] = pair


def to_step(groups, got_ref, count_ref, keep_ref, share_ref, out_ref, grad_ref):
    feats = got_ref.shape[0] // groups
    half = got_ref.shape[2] - LANES
    cross, second_sq = 0.0, 0.0
    for s in range(groups):
        parts = [got_ref[f * groups + s].astype(f32) for f in range(feats)]
        while len(parts) > 1:
            parts = [a + b for a, b in zip(parts[::2], parts[1::2])]
        cross = cross + parts[0][:, half:]
        second_sq = second_sq + parts[0][:, :half] * parts[0][:, :half]
    cross, second_sq = (jnp.sum(row_sum(v), axis=0, keepdims=True) for v in (cross, second_sq))
    count, sq_norm = count_ref[:, :1], keep_ref[:, 2 * LANES : 2 * LANES + 1]
    first_step, first_sq = keep_ref[:, :1], keep_ref[:, LANES : LANES + 1]
    sq_next = jnp.maximum(-first_step * cross / count, 0.0)
    beta = sq_next / sq_norm
    bend = jnp.maximum(second_sq + 2.0 * beta * cross + beta * beta * first_sq, 0.0)
    below = bend / count + penalty * (sq_next + beta * beta * sq_norm)
    step = jnp.where(sq_next > 0.0, sq_next / jnp.where(sq_next > 0.0, below, 1.0), 0.0)
    grad_ref[...] = share_ref[...]
    direction = -share_ref[...]
    out_ref[...] = first_step * direction + step * (keep_ref[:, 3 * LANES :] + beta * direction)


def exchange(values, axis, groups=None):
    return lax.all_to_all(
        values, axis, split_axis=0, concat_axis=0, tiled=True, axis_index_groups=groups
    )


def shards(embeddings, plant_ids, labels, weights):
    rows_here, width = embeddings.shape
    samps = lax.axis_size("samp")
    share = width // samps
    cap = 2 * rows_here // PEERS
    slots = PEERS * cap

    sent = call(
        functools.partial(pack_rows, cap),
        *(
            pltpu.with_memory_space_constraint(v, pltpu.HBM)
            for v in (plant_ids.reshape(1, rows_here), labels.reshape(1, rows_here), embeddings)
        ),
        out=shape(PEERS, cap // DEEP * (width // LANES) + 1, DEEP, LANES, dtype=bf16),
        scratch=(
            pltpu.VMEM((1, rows_here), jnp.int32),
            pltpu.VMEM((1, rows_here), jnp.int32),
            pltpu.VMEM((rows_here, width), bf16),
            pltpu.SemaphoreType.DMA((3,)),
        ),
        space=pltpu.HBM,
    )
    got = exchange(sent, "plant")
    rows, tags, part = call(
        functools.partial(take_rows, cap),
        got,
        weights,
        out=(shape(slots, width, dtype=bf16), shape(1, slots), shape(PEERS, 1, slots)),
    )
    got = exchange(part, "feat")
    curv, part = call(
        to_residual, got, tags, rows, out=(shape(1, slots), shape(PEERS, 1, width + LANES))
    )
    got = exchange(part, "samp")
    grad, count, grad_share, part = call(
        to_direction,
        got,
        weights,
        rows,
        out=(
            shape(1, width),
            shape(1, LANES),
            shape(1, share),
            shape(PEERS, 1, slots + LANES),
        ),
    )
    got = exchange(part, "feat")
    proj, part = call(
        to_image, got, curv, rows, out=(shape(1, slots + LANES), shape(PEERS, 1, width + LANES))
    )
    got = exchange(part, "samp")
    pair = (2, slots // 2 + LANES)
    keep, part = call(
        to_second,
        got,
        proj,
        curv,
        grad,
        count,
        rows,
        out=(
            shape(1, 3 * LANES + share),
            shape(lax.axis_size("feat") * samps, *pair, dtype=bf16),
        ),
        scratch=(pltpu.VMEM(pair, f32),),
    )
    feats = lax.axis_size("feat")
    runs = [(f ^ 1) * samps + s for f in range(feats) for s in range(samps)]
    got = exchange(part, ("feat", "samp"), [runs])
    return call(
        functools.partial(to_step, samps),
        got,
        count,
        keep,
        grad_share,
        out=(shape(1, share), shape(1, share)),
    )


def solution(mesh):
    placed = (
        P(("plant", "samp"), "feat"),
        P(("plant", "samp"), None),
        P(("plant", "samp")),
        P("plant", "feat"),
    )
    return jax.shard_map(
        shards,
        mesh=mesh,
        in_specs=placed,
        out_specs=(P("plant", ("feat", "samp")), P("plant", ("feat", "samp"))),
        check_vma=False,
    )
```

```python
import functools

import jax
import jax.numpy as jnp
from jax import lax
from jax.experimental import pallas as pl
from jax.experimental.pallas import tpu as pltpu
from jax.sharding import PartitionSpec as P

penalty = 0.1
PEERS = 8
LANES = 128
DEEP = 16
GRANT = 12 << 20
f32 = jnp.float32
bf16 = jnp.bfloat16


def nt(a, b):
    return lax.dot_general(a, b, (((1,), (1,)), ((), ())), preferred_element_type=f32)


def nn(a, b):
    return lax.dot_general(a, b, (((1,), (0,)), ((), ())), preferred_element_type=f32)


def rep(row):
    return jnp.broadcast_to(row, (PEERS, row.shape[1]))


def total_of(ref):
    parts = [ref[p] for p in range(PEERS)]
    while len(parts) > 1:
        parts = [a + b for a, b in zip(parts[::2], parts[1::2])]
    return parts[0]


def send(ref, *rows):
    at = 0
    for row in rows:
        for p in range(PEERS):
            ref[p, :, at : at + row.shape[1]] = row
        at = at + row.shape[1]


def lanes(scalar):
    return jnp.broadcast_to(scalar, (1, LANES))


def row_sum(row):
    return jnp.sum(row, axis=1, keepdims=True)


def call(kernel, *args, out, scratch=(), space=pltpu.VMEM):
    return pl.pallas_call(
        kernel,
        out_shape=out,
        in_specs=[pl.BlockSpec(memory_space=space)] * len(args),
        scratch_shapes=scratch,
        out_specs=jax.tree.map(lambda _: pl.BlockSpec(memory_space=pltpu.VMEM), out),
        compiler_params=pltpu.CompilerParams(vmem_limit_bytes=GRANT),
        name=kernel.func.__name__ if isinstance(kernel, functools.partial) else kernel.__name__,
    )(*args)


def shape(*dims, dtype=f32):
    return jax.ShapeDtypeStruct(dims, dtype)


def pack_rows(cap, ids_in, lab_in, emb_in, out_ref, ids_ref, lab_ref, emb_ref, sems):
    copies = [
        pltpu.make_async_copy(src, dst, sems.at[k])
        for k, (src, dst) in enumerate(
            ((ids_in, ids_ref), (lab_in, lab_ref), (emb_in, emb_ref))
        )
    ]
    for copy in copies:
        copy.start()
    rows = emb_ref.shape[0]
    heads = lax.broadcasted_iota(jnp.int32, (PEERS, rows), 0)
    earlier = lax.broadcasted_iota(jnp.int32, (rows, rows), 0) < lax.broadcasted_iota(
        jnp.int32, (rows, rows), 1
    )
    earlier = earlier.astype(f32).astype(bf16)
    copies[0].wait()
    copies[1].wait()
    ids = ids_ref[...]
    mem_f = (heads == ids).astype(f32)
    before = nn(mem_f.astype(bf16), earlier)
    rank = jnp.sum(before * mem_f, axis=0, keepdims=True).astype(jnp.int32)
    at_rank = lax.broadcasted_iota(jnp.int32, (cap, rows), 0) == rank
    tags = (lab_ref[...] + 1).astype(f32)
    tag_slots = nt((mem_f * tags).astype(bf16), at_rank.astype(f32).astype(bf16))
    copies[2].wait()
    emb = emb_ref[...]
    across = emb.shape[1] // LANES
    for p in range(PEERS):
        pick = (at_rank & (ids == p)).astype(f32).astype(bf16)
        picked = nn(pick, emb).astype(bf16)
        for down in range(cap // DEEP):
            for over in range(across):
                out_ref[p, down * across + over] = picked[
                    down * DEEP : (down + 1) * DEEP, over * LANES : (over + 1) * LANES
                ]
        out_ref[p, cap // DEEP * across] = jnp.broadcast_to(
            tag_slots[p : p + 1], (DEEP, cap)
        ).astype(bf16)


def take_rows(cap, got_ref, w_ref, rows_ref, tags_ref, out_ref):
    across = rows_ref.shape[1] // LANES
    for p in range(PEERS):
        for down in range(cap // DEEP):
            for over in range(across):
                at = p * cap + down * DEEP
                rows_ref[at : at + DEEP, over * LANES : (over + 1) * LANES] = got_ref[
                    p, down * across + over
                ]
        tags_ref[:, p * cap : (p + 1) * cap] = got_ref[p, cap // DEEP * across].astype(f32)[:1]
    send(out_ref, nt(rep(w_ref[...]).astype(bf16), rows_ref[...])[:1])


def to_residual(got_ref, tags_ref, rows_ref, curv_ref, out_ref):
    logits = total_of(got_ref)
    tags = tags_ref[...]
    valid = tags > 0.0
    prob = jax.nn.sigmoid(logits)
    residual = jnp.where(valid, prob - jnp.maximum(tags - 1.0, 0.0), 0.0)
    curv_ref[...] = jnp.where(valid, prob * (1.0 - prob), 0.0)
    part = nn(rep(residual).astype(bf16), rows_ref[...])[:1]
    send(out_ref, part, lanes(row_sum(valid.astype(f32))))


def own_share(row, share):
    width = row.shape[1]
    at = lax.axis_index("samp") * share
    return pltpu.roll(row, lax.rem(width - at, width), 1)[:, :share]


def to_direction(got_ref, w_ref, rows_ref, grad_ref, count_ref, share_ref, out_ref):
    width = rows_ref.shape[1]
    total = total_of(got_ref)
    count = total[:, width : width + 1]
    grad = total[:, :width] / count + penalty * w_ref[...]
    grad_ref[...] = grad
    count_ref[...] = lanes(count)
    share_ref[...] = own_share(grad, share_ref.shape[1])
    part = nt(rep(-grad).astype(bf16), rows_ref[...])[:1]
    send(out_ref, part, lanes(row_sum(grad * grad)))


def to_image(got_ref, curv_ref, rows_ref, proj_ref, out_ref):
    slots = rows_ref.shape[0]
    total = total_of(got_ref)
    proj_ref[...] = total
    proj = total[:, :slots]
    weighted = (curv_ref[...] * proj).astype(bf16).astype(f32)
    part = nn(rep(weighted).astype(bf16), rows_ref[...])[:1]
    send(out_ref, part, lanes(row_sum(weighted * proj)))


def to_second(got_ref, proj_ref, curv_ref, grad_ref, count_ref, rows_ref, keep_ref, out_ref, pair_ref):
    width, slots = rows_ref.shape[1], rows_ref.shape[0]
    half = slots // 2
    total = total_of(got_ref)
    count = count_ref[:, :1]
    sq_norm = proj_ref[:, slots : slots + 1]
    direction = -grad_ref[...]
    image = total[:, :width] / count + penalty * direction
    bend = total[:, width : width + 1]
    step = sq_norm / (bend / count + penalty * sq_norm)
    resid = direction - step * image
    keep_ref[:, :LANES] = lanes(step)
    keep_ref[:, LANES : 2 * LANES] = lanes(bend)
    keep_ref[:, 2 * LANES : 3 * LANES] = lanes(sq_norm)
    keep_ref[:, 3 * LANES :] = own_share(resid, keep_ref.shape[1] - 3 * LANES)
    curv = curv_ref[...]
    part = nt(rep(resid).astype(bf16), rows_ref[...])[:1]
    cross = row_sum(curv * proj_ref[:, :slots] * part)
    scaled = part * jnp.sqrt(curv)
    first = cross.astype(bf16).astype(f32)
    second = (cross - first).astype(bf16).astype(f32)
    third = cross - first - second
    lane = lax.broadcasted_iota(jnp.int32, (1, LANES), 1)
    extra = jnp.where(lane == 0, first, jnp.where(lane == 1, second, jnp.where(lane == 2, third, 0.0)))
    pair_ref[0:1, :half] = scaled[:, :half]
    pair_ref[1:2, :half] = scaled[:, half:]
    pair_ref[0:1, half:] = extra
    pair_ref[1:2, half:] = jnp.zeros((1, LANES), f32)
    pair = pair_ref[...].astype(bf16)
    for peer in range(out_ref.shape[0]):
        out_ref[peer] = pair


def to_step(groups, got_ref, count_ref, keep_ref, share_ref, out_ref, grad_ref):
    feats = got_ref.shape[0] // groups
    half = got_ref.shape[2] - LANES
    cross, second_sq = 0.0, 0.0
    for s in range(groups):
        parts = [got_ref[run * groups + s].astype(f32) for run in range(feats)]
        while len(parts) > 1:
            parts = [a + b for a, b in zip(parts[::2], parts[1::2])]
        cross = cross + parts[0][:, half:]
        second_sq = second_sq + parts[0][:, :half] * parts[0][:, :half]
    cross, second_sq = (jnp.sum(row_sum(v), axis=0, keepdims=True) for v in (cross, second_sq))
    count, sq_norm = count_ref[:, :1], keep_ref[:, 2 * LANES : 2 * LANES + 1]
    first_step, first_sq = keep_ref[:, :1], keep_ref[:, LANES : LANES + 1]
    sq_next = jnp.maximum(-first_step * cross / count, 0.0)
    beta = sq_next / sq_norm
    bend = jnp.maximum(second_sq + 2.0 * beta * cross + beta * beta * first_sq, 0.0)
    below = bend / count + penalty * (sq_next + beta * beta * sq_norm)
    step = jnp.where(sq_next > 0.0, sq_next / jnp.where(sq_next > 0.0, below, 1.0), 0.0)
    grad_ref[...] = share_ref[...]
    direction = -share_ref[...]
    out_ref[...] = first_step * direction + step * (keep_ref[:, 3 * LANES :] + beta * direction)


def exchange(values, axis, groups=None):
    return lax.all_to_all(
        values, axis, split_axis=0, concat_axis=0, tiled=True, axis_index_groups=groups
    )


def shards(embeddings, plant_ids, labels, weights):
    rows_here, width = embeddings.shape
    samps = lax.axis_size("samp")
    share = width // samps
    cap = 2 * rows_here // PEERS
    slots = PEERS * cap

    sent = call(
        functools.partial(pack_rows, cap),
        *(
            pltpu.with_memory_space_constraint(v, pltpu.HBM)
            for v in (plant_ids.reshape(1, rows_here), labels.reshape(1, rows_here), embeddings)
        ),
        out=shape(PEERS, cap // DEEP * (width // LANES) + 1, DEEP, LANES, dtype=bf16),
        scratch=(
            pltpu.VMEM((1, rows_here), jnp.int32),
            pltpu.VMEM((1, rows_here), jnp.int32),
            pltpu.VMEM((rows_here, width), bf16),
            pltpu.SemaphoreType.DMA((3,)),
        ),
        space=pltpu.HBM,
    )
    got = exchange(sent, "plant")
    rows, tags, part = call(
        functools.partial(take_rows, cap),
        got,
        weights,
        out=(shape(slots, width, dtype=bf16), shape(1, slots), shape(PEERS, 1, slots)),
    )
    got = exchange(part, "feat")
    curv, part = call(
        to_residual, got, tags, rows, out=(shape(1, slots), shape(PEERS, 1, width + LANES))
    )
    got = exchange(part, "samp")
    grad, count, grad_share, part = call(
        to_direction,
        got,
        weights,
        rows,
        out=(
            shape(1, width),
            shape(1, LANES),
            shape(1, share),
            shape(PEERS, 1, slots + LANES),
        ),
    )
    got = exchange(part, "feat")
    proj, part = call(
        to_image, got, curv, rows, out=(shape(1, slots + LANES), shape(PEERS, 1, width + LANES))
    )
    got = exchange(part, "samp")
    pair = (2, slots // 2 + LANES)
    keep, part = call(
        to_second,
        got,
        proj,
        curv,
        grad,
        count,
        rows,
        out=(
            shape(1, 3 * LANES + share),
            shape(lax.axis_size("feat") * samps, *pair, dtype=bf16),
        ),
        scratch=(pltpu.VMEM(pair, f32),),
    )
    feats = lax.axis_size("feat")
    runs = [f * samps + s for core in (0, 1) for f in range(core, feats, 2) for s in range(samps)]
    got = exchange(part, ("feat", "samp"), [runs])
    return call(
        functools.partial(to_step, samps),
        got,
        count,
        keep,
        grad_share,
        out=(shape(1, share), shape(1, share)),
    )


def solution(mesh):
    placed = (
        P(("plant", "samp"), "feat"),
        P(("plant", "samp"), None),
        P(("plant", "samp")),
        P("plant", "feat"),
    )
    return jax.shard_map(
        shards,
        mesh=mesh,
        in_specs=placed,
        out_specs=(P("plant", ("feat", "samp")), P("plant", ("feat", "samp"))),
        check_vma=False,
    )
```

```python
import functools

import jax
import jax.numpy as jnp
from jax import lax
from jax.experimental import pallas as pl
from jax.experimental.pallas import tpu as pltpu
from jax.sharding import PartitionSpec as P

penalty = 0.1
PEERS = 8
LANES = 128
DEEP = 16
GRANT = 12 << 20
f32 = jnp.float32
bf16 = jnp.bfloat16


def nt(a, b):
    return lax.dot_general(a, b, (((1,), (1,)), ((), ())), preferred_element_type=f32)


def nn(a, b):
    return lax.dot_general(a, b, (((1,), (0,)), ((), ())), preferred_element_type=f32)


def rep(row):
    return jnp.broadcast_to(row, (PEERS, row.shape[1]))


def total_of(ref):
    parts = [ref[p] for p in range(PEERS)]
    while len(parts) > 1:
        parts = [a + b for a, b in zip(parts[::2], parts[1::2])]
    return parts[0]


def send(ref, *rows):
    at = 0
    for row in rows:
        for p in range(PEERS):
            ref[p, :, at : at + row.shape[1]] = row
        at = at + row.shape[1]


def lanes(scalar):
    return jnp.broadcast_to(scalar, (1, LANES))


def row_sum(row):
    return jnp.sum(row, axis=1, keepdims=True)


def call(kernel, *args, out, scratch=(), space=pltpu.VMEM):
    return pl.pallas_call(
        kernel,
        out_shape=out,
        in_specs=[pl.BlockSpec(memory_space=space)] * len(args),
        scratch_shapes=scratch,
        out_specs=jax.tree.map(lambda _: pl.BlockSpec(memory_space=pltpu.VMEM), out),
        compiler_params=pltpu.CompilerParams(vmem_limit_bytes=GRANT),
        name=kernel.func.__name__ if isinstance(kernel, functools.partial) else kernel.__name__,
    )(*args)


def shape(*dims, dtype=f32):
    return jax.ShapeDtypeStruct(dims, dtype)


def pack_rows(cap, ids_in, lab_in, emb_in, out_ref, ids_ref, lab_ref, emb_ref, sems):
    copies = [
        pltpu.make_async_copy(src, dst, sems.at[k])
        for k, (src, dst) in enumerate(
            ((ids_in, ids_ref), (lab_in, lab_ref), (emb_in, emb_ref))
        )
    ]
    for copy in copies:
        copy.start()
    rows = emb_ref.shape[0]
    heads = lax.broadcasted_iota(jnp.int32, (PEERS, rows), 0)
    earlier = lax.broadcasted_iota(jnp.int32, (rows, rows), 0) < lax.broadcasted_iota(
        jnp.int32, (rows, rows), 1
    )
    earlier = earlier.astype(f32).astype(bf16)
    copies[0].wait()
    copies[1].wait()
    ids = ids_ref[...]
    mem_f = (heads == ids).astype(f32)
    before = nn(mem_f.astype(bf16), earlier)
    rank = jnp.sum(before * mem_f, axis=0, keepdims=True).astype(jnp.int32)
    at_rank = lax.broadcasted_iota(jnp.int32, (cap, rows), 0) == rank
    tags = (lab_ref[...] + 1).astype(f32)
    tag_slots = nt((mem_f * tags).astype(bf16), at_rank.astype(f32).astype(bf16))
    copies[2].wait()
    emb = emb_ref[...]
    across = emb.shape[1] // LANES
    for p in range(PEERS):
        pick = (at_rank & (ids == p)).astype(f32).astype(bf16)
        picked = nn(pick, emb).astype(bf16)
        for down in range(cap // DEEP):
            for over in range(across):
                out_ref[p, down * across + over] = picked[
                    down * DEEP : (down + 1) * DEEP, over * LANES : (over + 1) * LANES
                ]
        out_ref[p, cap // DEEP * across] = jnp.broadcast_to(
            tag_slots[p : p + 1], (DEEP, cap)
        ).astype(bf16)


def take_rows(cap, got_ref, w_ref, rows_ref, tags_ref, out_ref):
    across = rows_ref.shape[1] // LANES
    for p in range(PEERS):
        for down in range(cap // DEEP):
            for over in range(across):
                at = p * cap + down * DEEP
                rows_ref[at : at + DEEP, over * LANES : (over + 1) * LANES] = got_ref[
                    p, down * across + over
                ]
        tags_ref[:, p * cap : (p + 1) * cap] = got_ref[p, cap // DEEP * across].astype(f32)[:1]
    send(out_ref, nt(rep(w_ref[...]).astype(bf16), rows_ref[...])[:1])


def to_residual(got_ref, tags_ref, rows_ref, curv_ref, out_ref):
    logits = total_of(got_ref)
    tags = tags_ref[...]
    valid = tags > 0.0
    prob = jax.nn.sigmoid(logits)
    residual = jnp.where(valid, prob - jnp.maximum(tags - 1.0, 0.0), 0.0)
    curv_ref[...] = jnp.where(valid, prob * (1.0 - prob), 0.0)
    part = nn(rep(residual).astype(bf16), rows_ref[...])[:1]
    send(out_ref, part, lanes(row_sum(valid.astype(f32))))


def own_share(row, share):
    width = row.shape[1]
    at = lax.axis_index("samp") * share
    return pltpu.roll(row, lax.rem(width - at, width), 1)[:, :share]


def to_direction(got_ref, w_ref, rows_ref, grad_ref, count_ref, share_ref, out_ref):
    width = rows_ref.shape[1]
    total = total_of(got_ref)
    count = total[:, width : width + 1]
    grad = total[:, :width] / count + penalty * w_ref[...]
    grad_ref[...] = grad
    count_ref[...] = lanes(count)
    share_ref[...] = own_share(grad, share_ref.shape[1])
    part = nt(rep(-grad).astype(bf16), rows_ref[...])[:1]
    send(out_ref, part, lanes(row_sum(grad * grad)))


def to_image(got_ref, curv_ref, rows_ref, proj_ref, out_ref):
    slots = rows_ref.shape[0]
    total = total_of(got_ref)
    proj_ref[...] = total
    proj = total[:, :slots]
    weighted = (curv_ref[...] * proj).astype(bf16).astype(f32)
    part = nn(rep(weighted).astype(bf16), rows_ref[...])[:1]
    send(out_ref, part, lanes(row_sum(weighted * proj)))


def to_second(got_ref, proj_ref, curv_ref, grad_ref, count_ref, rows_ref, keep_ref, out_ref, pair_ref):
    width, slots = rows_ref.shape[1], rows_ref.shape[0]
    half = slots // 2
    total = total_of(got_ref)
    count = count_ref[:, :1]
    sq_norm = proj_ref[:, slots : slots + 1]
    direction = -grad_ref[...]
    image = total[:, :width] / count + penalty * direction
    bend = total[:, width : width + 1]
    step = sq_norm / (bend / count + penalty * sq_norm)
    resid = direction - step * image
    keep_ref[:, :LANES] = lanes(step)
    keep_ref[:, LANES : 2 * LANES] = lanes(bend)
    keep_ref[:, 2 * LANES : 3 * LANES] = lanes(sq_norm)
    keep_ref[:, 3 * LANES :] = own_share(resid, keep_ref.shape[1] - 3 * LANES)
    curv = curv_ref[...]
    part = nt(rep(resid).astype(bf16), rows_ref[...])[:1]
    cross = row_sum(curv * proj_ref[:, :slots] * part)
    scaled = part * jnp.sqrt(curv)
    first = cross.astype(bf16).astype(f32)
    second = (cross - first).astype(bf16).astype(f32)
    third = cross - first - second
    lane = lax.broadcasted_iota(jnp.int32, (1, LANES), 1)
    extra = jnp.where(lane == 0, first, jnp.where(lane == 1, second, jnp.where(lane == 2, third, 0.0)))
    pair_ref[0:1, :half] = scaled[:, :half]
    pair_ref[1:2, :half] = scaled[:, half:]
    pair_ref[0:1, half:] = extra
    pair_ref[1:2, half:] = jnp.zeros((1, LANES), f32)
    pair = pair_ref[...].astype(bf16)
    for peer in range(out_ref.shape[0]):
        out_ref[peer] = pair


def to_step(groups, got_ref, count_ref, keep_ref, share_ref, out_ref, grad_ref):
    feats = got_ref.shape[0] // groups
    half = got_ref.shape[2] - LANES
    cross, second_sq = 0.0, 0.0
    for s in range(groups):
        parts = [got_ref[run * groups + s].astype(f32) for run in range(feats)]
        while len(parts) > 1:
            parts = [a + b for a, b in zip(parts[::2], parts[1::2])]
        cross = cross + parts[0][:, half:]
        second_sq = second_sq + parts[0][:, :half] * parts[0][:, :half]
    cross, second_sq = (jnp.sum(row_sum(v), axis=0, keepdims=True) for v in (cross, second_sq))
    count, sq_norm = count_ref[:, :1], keep_ref[:, 2 * LANES : 2 * LANES + 1]
    first_step, first_sq = keep_ref[:, :1], keep_ref[:, LANES : LANES + 1]
    sq_next = jnp.maximum(-first_step * cross / count, 0.0)
    beta = sq_next / sq_norm
    bend = jnp.maximum(second_sq + 2.0 * beta * cross + beta * beta * first_sq, 0.0)
    below = bend / count + penalty * (sq_next + beta * beta * sq_norm)
    step = jnp.where(sq_next > 0.0, sq_next / jnp.where(sq_next > 0.0, below, 1.0), 0.0)
    grad_ref[...] = share_ref[...]
    direction = -share_ref[...]
    out_ref[...] = first_step * direction + step * (keep_ref[:, 3 * LANES :] + beta * direction)


def exchange(values, axis, groups=None):
    return lax.all_to_all(
        values, axis, split_axis=0, concat_axis=0, tiled=True, axis_index_groups=groups
    )


def shards(embeddings, plant_ids, labels, weights):
    rows_here, width = embeddings.shape
    samps = lax.axis_size("samp")
    share = width // samps
    cap = 2 * rows_here // PEERS
    slots = PEERS * cap

    sent = call(
        functools.partial(pack_rows, cap),
        *(
            pltpu.with_memory_space_constraint(v, pltpu.HBM)
            for v in (plant_ids.reshape(1, rows_here), labels.reshape(1, rows_here), embeddings)
        ),
        out=shape(PEERS, cap // DEEP * (width // LANES) + 1, DEEP, LANES, dtype=bf16),
        scratch=(
            pltpu.VMEM((1, rows_here), jnp.int32),
            pltpu.VMEM((1, rows_here), jnp.int32),
            pltpu.VMEM((rows_here, width), bf16),
            pltpu.SemaphoreType.DMA((3,)),
        ),
        space=pltpu.HBM,
    )
    got = exchange(sent, "plant")
    rows, tags, part = call(
        functools.partial(take_rows, cap),
        got,
        weights,
        out=(shape(slots, width, dtype=bf16), shape(1, slots), shape(PEERS, 1, slots)),
    )
    got = exchange(part, "feat")
    curv, part = call(
        to_residual, got, tags, rows, out=(shape(1, slots), shape(PEERS, 1, width + LANES))
    )
    got = exchange(part, "samp")
    grad, count, grad_share, part = call(
        to_direction,
        got,
        weights,
        rows,
        out=(
            shape(1, width),
            shape(1, LANES),
            shape(1, share),
            shape(PEERS, 1, slots + LANES),
        ),
    )
    got = exchange(part, "feat")
    proj, part = call(
        to_image, got, curv, rows, out=(shape(1, slots + LANES), shape(PEERS, 1, width + LANES))
    )
    got = exchange(part, "samp")
    pair = (2, slots // 2 + LANES)
    keep, part = call(
        to_second,
        got,
        proj,
        curv,
        grad,
        count,
        rows,
        out=(
            shape(1, 3 * LANES + share),
            shape(lax.axis_size("feat") * samps, *pair, dtype=bf16),
        ),
        scratch=(pltpu.VMEM(pair, f32),),
    )
    feats = lax.axis_size("feat")
    runs = [
        (f + core) * samps + s
        for f in range(feats - 2, -1, -2)
        for core in (0, 1)
        for s in range(samps)
    ]
    got = exchange(part, ("feat", "samp"), [runs])
    return call(
        functools.partial(to_step, samps),
        got,
        count,
        keep,
        grad_share,
        out=(shape(1, share), shape(1, share)),
    )


def solution(mesh):
    placed = (
        P(("plant", "samp"), "feat"),
        P(("plant", "samp"), None),
        P(("plant", "samp")),
        P("plant", "feat"),
    )
    return jax.shard_map(
        shards,
        mesh=mesh,
        in_specs=placed,
        out_specs=(P("plant", ("feat", "samp")), P("plant", ("feat", "samp"))),
        check_vma=False,
    )
```

```python
import functools

import jax
import jax.numpy as jnp
from jax import lax
from jax.experimental import pallas as pl
from jax.experimental.pallas import tpu as pltpu
from jax.sharding import PartitionSpec as P

penalty = 0.1
PEERS = 8
SPREAD = (0, 4, 2, 6, 1, 5, 3, 7)
LANES = 128
DEEP = 16
GRANT = 12 << 20
f32 = jnp.float32
bf16 = jnp.bfloat16


def nt(a, b):
    return lax.dot_general(a, b, (((1,), (1,)), ((), ())), preferred_element_type=f32)


def nn(a, b):
    return lax.dot_general(a, b, (((1,), (0,)), ((), ())), preferred_element_type=f32)


def rep(row):
    return jnp.broadcast_to(row, (PEERS, row.shape[1]))


def total_of(ref):
    parts = [ref[p] for p in range(PEERS)]
    while len(parts) > 1:
        parts = [a + b for a, b in zip(parts[::2], parts[1::2])]
    return parts[0]


def send(ref, *rows):
    at = 0
    for row in rows:
        for p in range(PEERS):
            ref[p, :, at : at + row.shape[1]] = row
        at = at + row.shape[1]


def lanes(scalar):
    return jnp.broadcast_to(scalar, (1, LANES))


def row_sum(row):
    return jnp.sum(row, axis=1, keepdims=True)


def call(kernel, *args, out, scratch=(), space=pltpu.VMEM):
    return pl.pallas_call(
        kernel,
        out_shape=out,
        in_specs=[pl.BlockSpec(memory_space=space)] * len(args),
        scratch_shapes=scratch,
        out_specs=jax.tree.map(lambda _: pl.BlockSpec(memory_space=pltpu.VMEM), out),
        compiler_params=pltpu.CompilerParams(vmem_limit_bytes=GRANT),
        name=kernel.func.__name__ if isinstance(kernel, functools.partial) else kernel.__name__,
    )(*args)


def shape(*dims, dtype=f32):
    return jax.ShapeDtypeStruct(dims, dtype)


def pack_rows(cap, ids_in, lab_in, emb_in, out_ref, ids_ref, lab_ref, emb_ref, sems):
    copies = [
        pltpu.make_async_copy(src, dst, sems.at[k])
        for k, (src, dst) in enumerate(
            ((ids_in, ids_ref), (lab_in, lab_ref), (emb_in, emb_ref))
        )
    ]
    for copy in copies:
        copy.start()
    rows = emb_ref.shape[0]
    heads = lax.broadcasted_iota(jnp.int32, (PEERS, rows), 0)
    earlier = lax.broadcasted_iota(jnp.int32, (rows, rows), 0) < lax.broadcasted_iota(
        jnp.int32, (rows, rows), 1
    )
    earlier = earlier.astype(f32).astype(bf16)
    copies[0].wait()
    copies[1].wait()
    ids = ids_ref[...]
    mem_f = (heads == ids).astype(f32)
    before = nn(mem_f.astype(bf16), earlier)
    rank = jnp.sum(before * mem_f, axis=0, keepdims=True).astype(jnp.int32)
    at_rank = lax.broadcasted_iota(jnp.int32, (cap, rows), 0) == rank
    tags = (lab_ref[...] + 1).astype(f32)
    tag_slots = nt((mem_f * tags).astype(bf16), at_rank.astype(f32).astype(bf16))
    copies[2].wait()
    emb = emb_ref[...]
    across = emb.shape[1] // LANES
    for at, p in enumerate(SPREAD):
        pick = (at_rank & (ids == p)).astype(f32).astype(bf16)
        picked = nn(pick, emb).astype(bf16)
        for down in range(cap // DEEP):
            for over in range(across):
                out_ref[at, down * across + over] = picked[
                    down * DEEP : (down + 1) * DEEP, over * LANES : (over + 1) * LANES
                ]
        out_ref[at, cap // DEEP * across] = jnp.broadcast_to(
            tag_slots[p : p + 1], (DEEP, cap)
        ).astype(bf16)


def take_rows(cap, got_ref, w_ref, rows_ref, tags_ref, out_ref):
    across = rows_ref.shape[1] // LANES
    for p in range(PEERS):
        for down in range(cap // DEEP):
            for over in range(across):
                at = p * cap + down * DEEP
                rows_ref[at : at + DEEP, over * LANES : (over + 1) * LANES] = got_ref[
                    p, down * across + over
                ]
        tags_ref[:, p * cap : (p + 1) * cap] = got_ref[p, cap // DEEP * across].astype(f32)[:1]
    send(out_ref, nt(rep(w_ref[...]).astype(bf16), rows_ref[...])[:1])


def to_residual(got_ref, tags_ref, rows_ref, curv_ref, out_ref):
    logits = total_of(got_ref)
    tags = tags_ref[...]
    valid = tags > 0.0
    prob = jax.nn.sigmoid(logits)
    residual = jnp.where(valid, prob - jnp.maximum(tags - 1.0, 0.0), 0.0)
    curv_ref[...] = jnp.where(valid, prob * (1.0 - prob), 0.0)
    part = nn(rep(residual).astype(bf16), rows_ref[...])[:1]
    send(out_ref, part, lanes(row_sum(valid.astype(f32))))


def own_share(row, share):
    width = row.shape[1]
    at = lax.axis_index("samp") * share
    return pltpu.roll(row, lax.rem(width - at, width), 1)[:, :share]


def to_direction(got_ref, w_ref, rows_ref, grad_ref, count_ref, share_ref, out_ref):
    width = rows_ref.shape[1]
    total = total_of(got_ref)
    count = total[:, width : width + 1]
    grad = total[:, :width] / count + penalty * w_ref[...]
    grad_ref[...] = grad
    count_ref[...] = lanes(count)
    share_ref[...] = own_share(grad, share_ref.shape[1])
    part = nt(rep(-grad).astype(bf16), rows_ref[...])[:1]
    send(out_ref, part, lanes(row_sum(grad * grad)))


def to_image(got_ref, curv_ref, rows_ref, sq_norm_ref, out_ref):
    slots = rows_ref.shape[0]
    total = total_of(got_ref)
    sq_norm_ref[...] = total[:, slots:]
    proj = total[:, :slots]
    curv = curv_ref[...]
    weighted = (curv * proj).astype(bf16).astype(f32)
    part = nn(rep(weighted).astype(bf16), rows_ref[...])[:1]
    send(out_ref, part, lanes(row_sum(weighted * proj)), jnp.sqrt(curv) * proj)


def to_second(got_ref, sq_norm_ref, curv_ref, grad_ref, count_ref, rows_ref, keep_ref, out_ref):
    width, cap = rows_ref.shape[1], rows_ref.shape[0] // PEERS
    total = got_ref[0, :, : width + LANES]
    for p in range(1, PEERS):
        total = total + got_ref[p, :, : width + LANES]
    count = count_ref[:, :1]
    sq_norm = sq_norm_ref[:, :1]
    direction = -grad_ref[...]
    image = total[:, :width] / count + penalty * direction
    step = sq_norm / (total[:, width : width + 1] / count + penalty * sq_norm)
    resid = direction - step * image
    keep_ref[:, :LANES] = lanes(step)
    keep_ref[:, LANES:] = own_share(resid, keep_ref.shape[1] - LANES)
    part = nt(rep(resid).astype(bf16), rows_ref[...]) * jnp.sqrt(curv_ref[...])
    source = lax.broadcasted_iota(jnp.int32, (PEERS, cap), 0)
    tile = part[:, :cap]
    for p in range(1, PEERS):
        tile = jnp.where(source == p, part[:, p * cap : (p + 1) * cap], tile)
    tile = tile.astype(bf16)
    for peer in range(out_ref.shape[0]):
        out_ref[peer] = tile


def to_step(got_ref, first_ref, count_ref, sq_norm_ref, keep_ref, share_ref, out_ref, grad_ref, tiles_ref):
    groups, _, cap = tiles_ref.shape
    feats = got_ref.shape[0] // groups
    start = first_ref.shape[2] - PEERS * cap
    for s in range(groups):
        for p in range(PEERS):
            tiles_ref[s, p : p + 1, :] = first_ref[s, :, start + p * cap : start + (p + 1) * cap]
    first_sq, cross, second_sq = 0.0, 0.0, 0.0
    for s in range(groups):
        first = tiles_ref[s]
        second = got_ref[s].astype(f32)
        for f in range(1, feats):
            second = second + got_ref[f * groups + s].astype(f32)
        first_sq = first_sq + first * first
        cross = cross + first * second
        second_sq = second_sq + second * second
    first_sq, cross, second_sq = (
        jnp.sum(row_sum(v), axis=0, keepdims=True) for v in (first_sq, cross, second_sq)
    )
    count, sq_norm, first_step = count_ref[:, :1], sq_norm_ref[:, :1], keep_ref[:, :1]
    sq_next = jnp.maximum(-first_step * cross / count, 0.0)
    beta = sq_next / sq_norm
    bend = jnp.maximum(second_sq + 2.0 * beta * cross + beta * beta * first_sq, 0.0)
    below = bend / count + penalty * (sq_next + beta * beta * sq_norm)
    step = jnp.where(sq_next > 0.0, sq_next / jnp.where(sq_next > 0.0, below, 1.0), 0.0)
    grad_ref[...] = share_ref[...]
    direction = -share_ref[...]
    out_ref[...] = first_step * direction + step * (keep_ref[:, LANES:] + beta * direction)


def exchange(values, axis, groups=None):
    return lax.all_to_all(
        values, axis, split_axis=0, concat_axis=0, tiled=True, axis_index_groups=groups
    )


def shards(embeddings, plant_ids, labels, weights):
    rows_here, width = embeddings.shape
    samps = lax.axis_size("samp")
    share = width // samps
    cap = 2 * rows_here // PEERS
    slots = PEERS * cap

    sent = call(
        functools.partial(pack_rows, cap),
        *(
            pltpu.with_memory_space_constraint(v, pltpu.HBM)
            for v in (plant_ids.reshape(1, rows_here), labels.reshape(1, rows_here), embeddings)
        ),
        out=shape(PEERS, cap // DEEP * (width // LANES) + 1, DEEP, LANES, dtype=bf16),
        scratch=(
            pltpu.VMEM((1, rows_here), jnp.int32),
            pltpu.VMEM((1, rows_here), jnp.int32),
            pltpu.VMEM((rows_here, width), bf16),
            pltpu.SemaphoreType.DMA((3,)),
        ),
        space=pltpu.HBM,
    )
    got = exchange(sent, "plant", [list(SPREAD)])
    rows, tags, part = call(
        functools.partial(take_rows, cap),
        got,
        weights,
        out=(shape(slots, width, dtype=bf16), shape(1, slots), shape(PEERS, 1, slots)),
    )
    got = exchange(part, "feat")
    curv, part = call(
        to_residual, got, tags, rows, out=(shape(1, slots), shape(PEERS, 1, width + LANES))
    )
    got = exchange(part, "samp")
    grad, count, grad_share, part = call(
        to_direction,
        got,
        weights,
        rows,
        out=(
            shape(1, width),
            shape(1, LANES),
            shape(1, share),
            shape(PEERS, 1, slots + LANES),
        ),
    )
    got = exchange(part, "feat")
    sq_norm, first = call(
        to_image,
        got,
        curv,
        rows,
        out=(shape(1, LANES), shape(PEERS, 1, width + LANES + slots)),
    )
    first = exchange(first, "samp")
    keep, part = call(
        to_second,
        first,
        sq_norm,
        curv,
        grad,
        count,
        rows,
        out=(
            shape(1, LANES + share),
            shape(lax.axis_size("feat") * samps, PEERS, cap, dtype=bf16),
        ),
    )
    got = exchange(part, ("feat", "samp"))
    return call(
        to_step,
        got,
        first,
        count,
        sq_norm,
        keep,
        grad_share,
        out=(shape(1, share), shape(1, share)),
        scratch=(pltpu.VMEM((samps, PEERS, cap), f32),),
    )


def solution(mesh):
    placed = (
        P(("plant", "samp"), "feat"),
        P(("plant", "samp"), None),
        P(("plant", "samp")),
        P("plant", "feat"),
    )
    return jax.shard_map(
        shards,
        mesh=mesh,
        in_specs=placed,
        out_specs=(P("plant", ("feat", "samp")), P("plant", ("feat", "samp"))),
        check_vma=False,
    )
```

```python
import functools

import jax
import jax.numpy as jnp
from jax import lax
from jax.experimental import pallas as pl
from jax.experimental.pallas import tpu as pltpu
from jax.sharding import PartitionSpec as P

penalty = 0.1
PEERS = 8
SPREAD = (0, 4, 2, 6, 1, 5, 3, 7)
LANES = 128
DEEP = 16
GRANT = 12 << 20
f32 = jnp.float32
bf16 = jnp.bfloat16


def nt(a, b):
    return lax.dot_general(a, b, (((1,), (1,)), ((), ())), preferred_element_type=f32)


def nn(a, b):
    return lax.dot_general(a, b, (((1,), (0,)), ((), ())), preferred_element_type=f32)


def rep(row):
    return jnp.broadcast_to(row, (PEERS, row.shape[1]))


def total_of(ref):
    parts = [ref[p] for p in range(PEERS)]
    while len(parts) > 1:
        parts = [a + b for a, b in zip(parts[::2], parts[1::2])]
    return parts[0]


def send(ref, *rows):
    at = 0
    for row in rows:
        for p in range(PEERS):
            ref[p, :, at : at + row.shape[1]] = row
        at = at + row.shape[1]


def lanes(scalar):
    return jnp.broadcast_to(scalar, (1, LANES))


def row_sum(row):
    return jnp.sum(row, axis=1, keepdims=True)


def call(kernel, *args, out, scratch=(), space=pltpu.VMEM):
    return pl.pallas_call(
        kernel,
        out_shape=out,
        in_specs=[pl.BlockSpec(memory_space=space)] * len(args),
        scratch_shapes=scratch,
        out_specs=jax.tree.map(lambda _: pl.BlockSpec(memory_space=pltpu.VMEM), out),
        compiler_params=pltpu.CompilerParams(vmem_limit_bytes=GRANT),
        name=kernel.func.__name__ if isinstance(kernel, functools.partial) else kernel.__name__,
    )(*args)


def shape(*dims, dtype=f32):
    return jax.ShapeDtypeStruct(dims, dtype)


def pack_rows(cap, ids_in, lab_in, emb_in, out_ref, ids_ref, lab_ref, emb_ref, sems):
    copies = [
        pltpu.make_async_copy(src, dst, sems.at[k])
        for k, (src, dst) in enumerate(
            ((ids_in, ids_ref), (lab_in, lab_ref), (emb_in, emb_ref))
        )
    ]
    for copy in copies:
        copy.start()
    rows = emb_ref.shape[0]
    heads = lax.broadcasted_iota(jnp.int32, (PEERS, rows), 0)
    earlier = lax.broadcasted_iota(jnp.int32, (rows, rows), 0) < lax.broadcasted_iota(
        jnp.int32, (rows, rows), 1
    )
    earlier = earlier.astype(f32).astype(bf16)
    copies[0].wait()
    copies[1].wait()
    ids = ids_ref[...]
    mem_f = (heads == ids).astype(f32)
    before = nn(mem_f.astype(bf16), earlier)
    rank = jnp.sum(before * mem_f, axis=0, keepdims=True).astype(jnp.int32)
    at_rank = lax.broadcasted_iota(jnp.int32, (cap, rows), 0) == rank
    tags = (lab_ref[...] + 1).astype(f32)
    tag_slots = nt((mem_f * tags).astype(bf16), at_rank.astype(f32).astype(bf16))
    copies[2].wait()
    emb = emb_ref[...]
    across = emb.shape[1] // LANES
    for p in range(PEERS):
        pick = (at_rank & (ids == p)).astype(f32).astype(bf16)
        picked = nn(pick, emb).astype(bf16)
        for down in range(cap // DEEP):
            for over in range(across):
                out_ref[p, down * across + over] = picked[
                    down * DEEP : (down + 1) * DEEP, over * LANES : (over + 1) * LANES
                ]
        out_ref[p, cap // DEEP * across] = jnp.broadcast_to(
            tag_slots[p : p + 1], (DEEP, cap)
        ).astype(bf16)


def take_rows(cap, got_ref, w_ref, rows_ref, tags_ref, out_ref):
    across = rows_ref.shape[1] // LANES
    for p in range(PEERS):
        for down in range(cap // DEEP):
            for over in range(across):
                at = p * cap + down * DEEP
                rows_ref[at : at + DEEP, over * LANES : (over + 1) * LANES] = got_ref[
                    p, down * across + over
                ]
        tags_ref[:, p * cap : (p + 1) * cap] = got_ref[p, cap // DEEP * across].astype(f32)[:1]
    send(out_ref, nt(rep(w_ref[...]).astype(bf16), rows_ref[...])[:1])


def to_residual(got_ref, tags_ref, rows_ref, curv_ref, out_ref):
    logits = total_of(got_ref)
    tags = tags_ref[...]
    valid = tags > 0.0
    prob = jax.nn.sigmoid(logits)
    residual = jnp.where(valid, prob - jnp.maximum(tags - 1.0, 0.0), 0.0)
    curv_ref[...] = jnp.where(valid, prob * (1.0 - prob), 0.0)
    part = nn(rep(residual).astype(bf16), rows_ref[...])[:1]
    send(out_ref, part, lanes(row_sum(valid.astype(f32))))


def own_share(row, share):
    width = row.shape[1]
    at = lax.axis_index("samp") * share
    return pltpu.roll(row, lax.rem(width - at, width), 1)[:, :share]


def to_direction(got_ref, w_ref, rows_ref, grad_ref, count_ref, share_ref, out_ref):
    width = rows_ref.shape[1]
    total = total_of(got_ref)
    count = total[:, width : width + 1]
    grad = total[:, :width] / count + penalty * w_ref[...]
    grad_ref[...] = grad
    count_ref[...] = lanes(count)
    share_ref[...] = own_share(grad, share_ref.shape[1])
    part = nt(rep(-grad).astype(bf16), rows_ref[...])[:1]
    send(out_ref, part, lanes(row_sum(grad * grad)))


def to_image(got_ref, curv_ref, rows_ref, sq_norm_ref, out_ref):
    slots = rows_ref.shape[0]
    total = total_of(got_ref)
    sq_norm_ref[...] = total[:, slots:]
    proj = total[:, :slots]
    curv = curv_ref[...]
    weighted = (curv * proj).astype(bf16).astype(f32)
    part = nn(rep(weighted).astype(bf16), rows_ref[...])[:1]
    send(out_ref, part, lanes(row_sum(weighted * proj)), jnp.sqrt(curv) * proj)


def to_second(got_ref, sq_norm_ref, curv_ref, grad_ref, count_ref, rows_ref, keep_ref, out_ref):
    width, cap = rows_ref.shape[1], rows_ref.shape[0] // PEERS
    total = got_ref[0, :, : width + LANES]
    for p in range(1, PEERS):
        total = total + got_ref[p, :, : width + LANES]
    count = count_ref[:, :1]
    sq_norm = sq_norm_ref[:, :1]
    direction = -grad_ref[...]
    image = total[:, :width] / count + penalty * direction
    step = sq_norm / (total[:, width : width + 1] / count + penalty * sq_norm)
    resid = direction - step * image
    keep_ref[:, :LANES] = lanes(step)
    keep_ref[:, LANES:] = own_share(resid, keep_ref.shape[1] - LANES)
    part = nt(rep(resid).astype(bf16), rows_ref[...]) * jnp.sqrt(curv_ref[...])
    source = lax.broadcasted_iota(jnp.int32, (PEERS, cap), 0)
    tile = part[:, :cap]
    for p in range(1, PEERS):
        tile = jnp.where(source == p, part[:, p * cap : (p + 1) * cap], tile)
    tile = tile.astype(bf16)
    for peer in range(out_ref.shape[0]):
        out_ref[peer] = tile


def to_step(got_ref, first_ref, count_ref, sq_norm_ref, keep_ref, share_ref, out_ref, grad_ref, tiles_ref):
    groups, _, cap = tiles_ref.shape
    feats = got_ref.shape[0] // groups
    start = first_ref.shape[2] - PEERS * cap
    for s in range(groups):
        for p in range(PEERS):
            tiles_ref[s, p : p + 1, :] = first_ref[s, :, start + p * cap : start + (p + 1) * cap]
    first_sq, cross, second_sq = 0.0, 0.0, 0.0
    for at, s in enumerate(SPREAD):
        first = tiles_ref[at]
        second = got_ref[s].astype(f32)
        for f in range(1, feats):
            second = second + got_ref[f * groups + s].astype(f32)
        first_sq = first_sq + first * first
        cross = cross + first * second
        second_sq = second_sq + second * second
    first_sq, cross, second_sq = (
        jnp.sum(row_sum(v), axis=0, keepdims=True) for v in (first_sq, cross, second_sq)
    )
    count, sq_norm, first_step = count_ref[:, :1], sq_norm_ref[:, :1], keep_ref[:, :1]
    sq_next = jnp.maximum(-first_step * cross / count, 0.0)
    beta = sq_next / sq_norm
    bend = jnp.maximum(second_sq + 2.0 * beta * cross + beta * beta * first_sq, 0.0)
    below = bend / count + penalty * (sq_next + beta * beta * sq_norm)
    step = jnp.where(sq_next > 0.0, sq_next / jnp.where(sq_next > 0.0, below, 1.0), 0.0)
    grad_ref[...] = share_ref[...]
    direction = -share_ref[...]
    out_ref[...] = first_step * direction + step * (keep_ref[:, LANES:] + beta * direction)


def exchange(values, axis, groups=None):
    return lax.all_to_all(
        values, axis, split_axis=0, concat_axis=0, tiled=True, axis_index_groups=groups
    )


def shards(embeddings, plant_ids, labels, weights):
    rows_here, width = embeddings.shape
    samps = lax.axis_size("samp")
    share = width // samps
    cap = 2 * rows_here // PEERS
    slots = PEERS * cap

    sent = call(
        functools.partial(pack_rows, cap),
        *(
            pltpu.with_memory_space_constraint(v, pltpu.HBM)
            for v in (plant_ids.reshape(1, rows_here), labels.reshape(1, rows_here), embeddings)
        ),
        out=shape(PEERS, cap // DEEP * (width // LANES) + 1, DEEP, LANES, dtype=bf16),
        scratch=(
            pltpu.VMEM((1, rows_here), jnp.int32),
            pltpu.VMEM((1, rows_here), jnp.int32),
            pltpu.VMEM((rows_here, width), bf16),
            pltpu.SemaphoreType.DMA((3,)),
        ),
        space=pltpu.HBM,
    )
    got = exchange(sent, "plant")
    rows, tags, part = call(
        functools.partial(take_rows, cap),
        got,
        weights,
        out=(shape(slots, width, dtype=bf16), shape(1, slots), shape(PEERS, 1, slots)),
    )
    got = exchange(part, "feat")
    curv, part = call(
        to_residual, got, tags, rows, out=(shape(1, slots), shape(PEERS, 1, width + LANES))
    )
    got = exchange(part, "samp", [list(SPREAD)])
    grad, count, grad_share, part = call(
        to_direction,
        got,
        weights,
        rows,
        out=(
            shape(1, width),
            shape(1, LANES),
            shape(1, share),
            shape(PEERS, 1, slots + LANES),
        ),
    )
    got = exchange(part, "feat")
    sq_norm, first = call(
        to_image,
        got,
        curv,
        rows,
        out=(shape(1, LANES), shape(PEERS, 1, width + LANES + slots)),
    )
    first = exchange(first, "samp", [list(SPREAD)])
    keep, part = call(
        to_second,
        first,
        sq_norm,
        curv,
        grad,
        count,
        rows,
        out=(
            shape(1, LANES + share),
            shape(lax.axis_size("feat") * samps, PEERS, cap, dtype=bf16),
        ),
    )
    got = exchange(part, ("feat", "samp"))
    return call(
        to_step,
        got,
        first,
        count,
        sq_norm,
        keep,
        grad_share,
        out=(shape(1, share), shape(1, share)),
        scratch=(pltpu.VMEM((samps, PEERS, cap), f32),),
    )


def solution(mesh):
    placed = (
        P(("plant", "samp"), "feat"),
        P(("plant", "samp"), None),
        P(("plant", "samp")),
        P("plant", "feat"),
    )
    return jax.shard_map(
        shards,
        mesh=mesh,
        in_specs=placed,
        out_specs=(P("plant", ("feat", "samp")), P("plant", ("feat", "samp"))),
        check_vma=False,
    )
```

```python
import functools

import jax
import jax.numpy as jnp
from jax import lax
from jax.experimental import pallas as pl
from jax.experimental.pallas import tpu as pltpu
from jax.sharding import PartitionSpec as P

penalty = 0.1
PEERS = 8
SPREAD = (0, 4, 2, 6, 1, 5, 3, 7)
LANES = 128
DEEP = 16
GRANT = 12 << 20
f32 = jnp.float32
bf16 = jnp.bfloat16


def nt(a, b):
    return lax.dot_general(a, b, (((1,), (1,)), ((), ())), preferred_element_type=f32)


def nn(a, b):
    return lax.dot_general(a, b, (((1,), (0,)), ((), ())), preferred_element_type=f32)


def rep(row):
    return jnp.broadcast_to(row, (PEERS, row.shape[1]))


def total_of(ref):
    parts = [ref[p] for p in range(PEERS)]
    while len(parts) > 1:
        parts = [a + b for a, b in zip(parts[::2], parts[1::2])]
    return parts[0]


def send(ref, *rows):
    at = 0
    for row in rows:
        for p in range(PEERS):
            ref[p, :, at : at + row.shape[1]] = row
        at = at + row.shape[1]


def lanes(scalar):
    return jnp.broadcast_to(scalar, (1, LANES))


def row_sum(row):
    return jnp.sum(row, axis=1, keepdims=True)


def call(kernel, *args, out, scratch=(), space=pltpu.VMEM):
    return pl.pallas_call(
        kernel,
        out_shape=out,
        in_specs=[pl.BlockSpec(memory_space=space)] * len(args),
        scratch_shapes=scratch,
        out_specs=jax.tree.map(lambda _: pl.BlockSpec(memory_space=pltpu.VMEM), out),
        compiler_params=pltpu.CompilerParams(vmem_limit_bytes=GRANT),
        name=kernel.func.__name__ if isinstance(kernel, functools.partial) else kernel.__name__,
    )(*args)


def shape(*dims, dtype=f32):
    return jax.ShapeDtypeStruct(dims, dtype)


def pack_rows(cap, ids_in, lab_in, emb_in, out_ref, ids_ref, lab_ref, emb_ref, sems):
    copies = [
        pltpu.make_async_copy(src, dst, sems.at[k])
        for k, (src, dst) in enumerate(
            ((ids_in, ids_ref), (lab_in, lab_ref), (emb_in, emb_ref))
        )
    ]
    for copy in copies:
        copy.start()
    rows = emb_ref.shape[0]
    heads = lax.broadcasted_iota(jnp.int32, (PEERS, rows), 0)
    earlier = lax.broadcasted_iota(jnp.int32, (rows, rows), 0) < lax.broadcasted_iota(
        jnp.int32, (rows, rows), 1
    )
    earlier = earlier.astype(f32).astype(bf16)
    copies[0].wait()
    copies[1].wait()
    ids = ids_ref[...]
    mem_f = (heads == ids).astype(f32)
    before = nn(mem_f.astype(bf16), earlier)
    rank = jnp.sum(before * mem_f, axis=0, keepdims=True).astype(jnp.int32)
    at_rank = lax.broadcasted_iota(jnp.int32, (cap, rows), 0) == rank
    tags = (lab_ref[...] + 1).astype(f32)
    tag_slots = nt((mem_f * tags).astype(bf16), at_rank.astype(f32).astype(bf16))
    copies[2].wait()
    emb = emb_ref[...]
    across = emb.shape[1] // LANES
    for at, p in enumerate(SPREAD):
        pick = (at_rank & (ids == p)).astype(f32).astype(bf16)
        picked = nn(pick, emb).astype(bf16)
        for down in range(cap // DEEP):
            for over in range(across):
                out_ref[at, down * across + over] = picked[
                    down * DEEP : (down + 1) * DEEP, over * LANES : (over + 1) * LANES
                ]
        out_ref[at, cap // DEEP * across] = jnp.broadcast_to(
            tag_slots[p : p + 1], (DEEP, cap)
        ).astype(bf16)


def take_rows(cap, got_ref, w_ref, rows_ref, tags_ref, out_ref):
    across = rows_ref.shape[1] // LANES
    for p in range(PEERS):
        for down in range(cap // DEEP):
            for over in range(across):
                at = p * cap + down * DEEP
                rows_ref[at : at + DEEP, over * LANES : (over + 1) * LANES] = got_ref[
                    p, down * across + over
                ]
        tags_ref[:, p * cap : (p + 1) * cap] = got_ref[p, cap // DEEP * across].astype(f32)[:1]
    send(out_ref, nt(rep(w_ref[...]).astype(bf16), rows_ref[...])[:1])


def to_residual(got_ref, tags_ref, rows_ref, curv_ref, out_ref):
    logits = total_of(got_ref)
    tags = tags_ref[...]
    valid = tags > 0.0
    prob = jax.nn.sigmoid(logits)
    residual = jnp.where(valid, prob - jnp.maximum(tags - 1.0, 0.0), 0.0)
    curv_ref[...] = jnp.where(valid, prob * (1.0 - prob), 0.0)
    part = nn(rep(residual).astype(bf16), rows_ref[...])[:1]
    send(out_ref, part, lanes(row_sum(valid.astype(f32))))


def own_share(row, share):
    width = row.shape[1]
    at = lax.axis_index("samp") * share
    return pltpu.roll(row, lax.rem(width - at, width), 1)[:, :share]


def to_direction(got_ref, w_ref, rows_ref, grad_ref, count_ref, share_ref, out_ref):
    width = rows_ref.shape[1]
    total = total_of(got_ref)
    count = total[:, width : width + 1]
    grad = total[:, :width] / count + penalty * w_ref[...]
    grad_ref[...] = grad
    count_ref[...] = lanes(count)
    share_ref[...] = own_share(grad, share_ref.shape[1])
    part = nt(rep(-grad).astype(bf16), rows_ref[...])[:1]
    send(out_ref, part, lanes(row_sum(grad * grad)))


def to_image(got_ref, curv_ref, rows_ref, sq_norm_ref, out_ref):
    slots = rows_ref.shape[0]
    total = total_of(got_ref)
    sq_norm_ref[...] = total[:, slots:]
    proj = total[:, :slots]
    curv = curv_ref[...]
    weighted = (curv * proj).astype(bf16).astype(f32)
    part = nn(rep(weighted).astype(bf16), rows_ref[...])[:1]
    send(out_ref, part, lanes(row_sum(weighted * proj)), jnp.sqrt(curv) * proj)


def to_second(got_ref, sq_norm_ref, curv_ref, grad_ref, count_ref, rows_ref, keep_ref, out_ref):
    width, cap = rows_ref.shape[1], rows_ref.shape[0] // PEERS
    total = got_ref[0, :, : width + LANES]
    for p in range(1, PEERS):
        total = total + got_ref[p, :, : width + LANES]
    count = count_ref[:, :1]
    sq_norm = sq_norm_ref[:, :1]
    direction = -grad_ref[...]
    image = total[:, :width] / count + penalty * direction
    step = sq_norm / (total[:, width : width + 1] / count + penalty * sq_norm)
    resid = direction - step * image
    keep_ref[:, :LANES] = lanes(step)
    keep_ref[:, LANES:] = own_share(resid, keep_ref.shape[1] - LANES)
    part = nt(rep(resid).astype(bf16), rows_ref[...]) * jnp.sqrt(curv_ref[...])
    source = lax.broadcasted_iota(jnp.int32, (PEERS, cap), 0)
    tile = part[:, :cap]
    for p in range(1, PEERS):
        tile = jnp.where(source == p, part[:, p * cap : (p + 1) * cap], tile)
    tile = tile.astype(bf16)
    for peer in range(out_ref.shape[0]):
        out_ref[peer] = tile


def to_step(got_ref, first_ref, count_ref, sq_norm_ref, keep_ref, share_ref, out_ref, grad_ref, tiles_ref):
    groups, _, cap = tiles_ref.shape
    feats = got_ref.shape[0] // groups
    start = first_ref.shape[2] - PEERS * cap
    for s in range(groups):
        for p in range(PEERS):
            tiles_ref[s, p : p + 1, :] = first_ref[s, :, start + p * cap : start + (p + 1) * cap]
    first_sq, cross, second_sq = 0.0, 0.0, 0.0
    for at, s in enumerate(SPREAD):
        first = tiles_ref[at]
        second = got_ref[s].astype(f32)
        for f in range(1, feats):
            second = second + got_ref[f * groups + s].astype(f32)
        first_sq = first_sq + first * first
        cross = cross + first * second
        second_sq = second_sq + second * second
    first_sq, cross, second_sq = (
        jnp.sum(row_sum(v), axis=0, keepdims=True) for v in (first_sq, cross, second_sq)
    )
    count, sq_norm, first_step = count_ref[:, :1], sq_norm_ref[:, :1], keep_ref[:, :1]
    sq_next = jnp.maximum(-first_step * cross / count, 0.0)
    beta = sq_next / sq_norm
    bend = jnp.maximum(second_sq + 2.0 * beta * cross + beta * beta * first_sq, 0.0)
    below = bend / count + penalty * (sq_next + beta * beta * sq_norm)
    step = jnp.where(sq_next > 0.0, sq_next / jnp.where(sq_next > 0.0, below, 1.0), 0.0)
    grad_ref[...] = share_ref[...]
    direction = -share_ref[...]
    out_ref[...] = first_step * direction + step * (keep_ref[:, LANES:] + beta * direction)


def exchange(values, axis, groups=None):
    return lax.all_to_all(
        values, axis, split_axis=0, concat_axis=0, tiled=True, axis_index_groups=groups
    )


def shards(embeddings, plant_ids, labels, weights):
    rows_here, width = embeddings.shape
    samps = lax.axis_size("samp")
    share = width // samps
    cap = 2 * rows_here // PEERS
    slots = PEERS * cap

    sent = call(
        functools.partial(pack_rows, cap),
        *(
            pltpu.with_memory_space_constraint(v, pltpu.HBM)
            for v in (plant_ids.reshape(1, rows_here), labels.reshape(1, rows_here), embeddings)
        ),
        out=shape(PEERS, cap // DEEP * (width // LANES) + 1, DEEP, LANES, dtype=bf16),
        scratch=(
            pltpu.VMEM((1, rows_here), jnp.int32),
            pltpu.VMEM((1, rows_here), jnp.int32),
            pltpu.VMEM((rows_here, width), bf16),
            pltpu.SemaphoreType.DMA((3,)),
        ),
        space=pltpu.HBM,
    )
    got = exchange(sent, "plant", [list(SPREAD)])
    rows, tags, part = call(
        functools.partial(take_rows, cap),
        got,
        weights,
        out=(shape(slots, width, dtype=bf16), shape(1, slots), shape(PEERS, 1, slots)),
    )
    got = exchange(part, "feat")
    curv, part = call(
        to_residual, got, tags, rows, out=(shape(1, slots), shape(PEERS, 1, width + LANES))
    )
    got = exchange(part, "samp", [list(SPREAD)])
    grad, count, grad_share, part = call(
        to_direction,
        got,
        weights,
        rows,
        out=(
            shape(1, width),
            shape(1, LANES),
            shape(1, share),
            shape(PEERS, 1, slots + LANES),
        ),
    )
    got = exchange(part, "feat")
    sq_norm, first = call(
        to_image,
        got,
        curv,
        rows,
        out=(shape(1, LANES), shape(PEERS, 1, width + LANES + slots)),
    )
    first = exchange(first, "samp", [list(SPREAD)])
    keep, part = call(
        to_second,
        first,
        sq_norm,
        curv,
        grad,
        count,
        rows,
        out=(
            shape(1, LANES + share),
            shape(lax.axis_size("feat") * samps, PEERS, cap, dtype=bf16),
        ),
    )
    got = exchange(part, ("feat", "samp"))
    return call(
        to_step,
        got,
        first,
        count,
        sq_norm,
        keep,
        grad_share,
        out=(shape(1, share), shape(1, share)),
        scratch=(pltpu.VMEM((samps, PEERS, cap), f32),),
    )


def solution(mesh):
    placed = (
        P(("plant", "samp"), "feat"),
        P(("plant", "samp"), None),
        P(("plant", "samp")),
        P("plant", "feat"),
    )
    return jax.shard_map(
        shards,
        mesh=mesh,
        in_specs=placed,
        out_specs=(P("plant", ("feat", "samp")), P("plant", ("feat", "samp"))),
        check_vma=False,
    )
```
